256 devices in a mesh: dp: 8 (over x, z_hi), expert: 32 (over z_lo, y, core).
Axes of the slice: x: 4, y: 4, z: 8 (z_hi: 2, z_lo: 4; z = z_hi * 4 + z_lo), core: 2. Of those that a mesh axis runs over, the one named last changes fastest.
Arguments:
- tokens: bfloat16 [32768, 5120], P(('dp', 'expert')), may hold values from -6 to 6
- cotangent: bfloat16 [32768, 5120], P(('dp', 'expert')), may hold values from -2 to 2
- picks: int32 [256, 32, 4], P(('dp', 'expert')), may hold values from 0 to 127, as said below
- gates: float32 [256, 32, 4], P(('dp', 'expert')), may hold values from 0.05 to 1
- w_gate: bfloat16 [32, 5120, 768], P('expert', 'dp'), may hold values from -0.078125 to 0.078125
- w_up: bfloat16 [32, 5120, 768], P('expert', 'dp'), may hold values from -0.078125 to 0.078125
- w_down: bfloat16 [32, 768, 5120], P('expert', None, 'dp'), may hold values from -0.21875 to 0.21875
Outputs:
- mixed: bfloat16 [32768, 5120], P(('dp', 'expert'))
- token_grad: bfloat16 [32768, 5120], P(('dp', 'expert'))
- gate_grad: float32 [256, 32, 4], P(('dp', 'expert'))
- grad_w_gate: bfloat16 [32, 5120, 768], P('expert', 'dp')
- grad_w_up: bfloat16 [32, 5120, 768], P('expert', 'dp')
- grad_w_down: bfloat16 [32, 768, 5120], P('expert', None, 'dp')
The draws below stay inside these ranges and needn't reach their ends.
Inputs may be any that keep to these rules, and one draw needn't show every extreme that they name: picks[d, e] holds 4 distinct token indices of device d; every expert takes exactly 4 tokens from every device.
All inputs are finite; a program needn't handle non-finite values.
Results may differ from the reference program's by a relative error of at most 0.02.
Values may be sent and summed in bfloat16 or wider, within the bound.
A program may use at most 64 MiB of HBM per device.

```python
import math
import jax
import jax.numpy as jnp
from jax import lax

D = 5120
FF = 768
TOK_DEV = 128
SLOT = 4
EXPERTS = 32
SOURCES = 256
TOKENS = 32768
N_DP = 8


def draw_picks(key, part):
    subkeys = jax.random.split(jax.random.fold_in(key, 17), SOURCES * EXPERTS)

    def pick_one(subkey):
        return jax.random.permutation(subkey, TOK_DEV)[:SLOT]
    chosen = jax.vmap(pick_one)(subkeys)
    return chosen.reshape(SOURCES, EXPERTS, SLOT).astype(jnp.int32)


def shard_levels(own_key, dims, cuts, low, top_value):
    def one(position, blocks):
        steps = jax.random.uniform(jax.random.fold_in(jax.random.fold_in(own_key, 6), position), (blocks,), jnp.float32, low / len(cuts), top_value / len(cuts))
        return jnp.repeat(jnp.exp(steps), dims[position] // blocks).reshape((-1,) + (1,) * (len(dims) - position - 1))

    gain = one(*cuts[0])
    for cut in cuts[1:]:
        gain = gain * one(*cut)
    return gain


def centred(key, shape, scale, bound, shards=(), held_as=jnp.bfloat16):
    level = shard_levels(key, shape, shards, -0.22, 0.18) if shards else 1.0
    drawn = jax.random.normal(key, shape, jnp.float32) * scale * level
    return jnp.minimum(jnp.maximum(drawn, -bound), bound).astype(held_as)


def setup_inputs(seed: int = 0) -> dict:
    key_list = jax.random.split(jax.random.key(seed), 8)
    return {
        "tokens": centred(key_list[0], (TOKENS, D), 1.0, 6.0, ((0, 256),)),
        "cotangent": centred(key_list[1], (TOKENS, D), 0.25, 2.0, ((0, 256),)),
        "picks": draw_picks(jax.random.fold_in(key_list[7], 71), 0),
        "gates": jnp.clip(jnp.exp(math.log(1.0) - 2.9957323 * jax.random.uniform(key_list[3], (SOURCES, EXPERTS, SLOT), jnp.float32) ** shard_levels(key_list[3], (SOURCES, EXPERTS, SLOT), ((0, 256),), -0.2, 0.2)), 0.05, 1.0),
        "w_gate": centred(key_list[4], (EXPERTS, D, FF), D ** -0.5, 0.078125, ((0, 32), (1, 8))),
        "w_up": centred(key_list[5], (EXPERTS, D, FF), D ** -0.5, 0.078125, ((0, 32), (1, 8))),
        "w_down": centred(key_list[6], (EXPERTS, FF, D), FF ** -0.5, 0.21875, ((0, 32), (2, 8))),
    }


def swiglu_grads(gate_sum, up_sum, back_sum):
    sigmoid_gate = jax.nn.sigmoid(gate_sum)
    silu_gate = gate_sum * sigmoid_gate
    hidden = (silu_gate * up_sum).astype(jnp.bfloat16)
    grad_up = (back_sum * silu_gate).astype(jnp.bfloat16)
    grad_gate = (back_sum * up_sum * sigmoid_gate * (1.0 + gate_sum * (1.0 - sigmoid_gate))).astype(jnp.bfloat16)
    return hidden, grad_gate, grad_up


def blockwise(form, left, right):
    parts = jnp.einsum(form, left, right, precision=lax.Precision.HIGHEST)
    parts = lax.optimization_barrier(parts.astype(jnp.bfloat16)).astype(jnp.float32)
    return jnp.sum(parts, axis=0)


def reference(tokens, cotangent, picks, gates, w_gate, w_up, w_down):
    sources = picks.shape[0]
    expert_count = picks.shape[1]
    slot_count = picks.shape[2]
    model_width = tokens.shape[1]
    per_device = tokens.shape[0] // sources
    hidden_units = w_gate.shape[2]
    slice_width = model_width // N_DP
    row_count = sources * slot_count
    offsets = (jnp.arange(sources, dtype=jnp.int32) * per_device)[:, None, None]
    flat_rows = (picks + offsets).astype(jnp.int32).reshape(-1)
    token_rows = jnp.take(tokens, flat_rows, axis=0).reshape(sources, expert_count, slot_count, model_width)
    grad_rows = jnp.take(cotangent, flat_rows, axis=0).reshape(sources, expert_count, slot_count, model_width)
    scaled = (gates[..., None] * grad_rows.astype(jnp.float32)).astype(jnp.bfloat16)
    by_expert_in = jnp.moveaxis(token_rows, 1, 0).reshape(expert_count, row_count, model_width)
    by_expert_up = jnp.moveaxis(scaled, 1, 0).reshape(expert_count, row_count, model_width)

    def one_expert(operands):
        rows_in, rows_up, gate_w, up_w, down_w = operands
        split_in = rows_in.astype(jnp.float32).reshape(row_count, N_DP, slice_width)
        split_up = rows_up.astype(jnp.float32).reshape(row_count, N_DP, slice_width)
        gate_blocks = gate_w.astype(jnp.float32).reshape(N_DP, slice_width, hidden_units)
        up_blocks = up_w.astype(jnp.float32).reshape(N_DP, slice_width, hidden_units)
        down_blocks = down_w.astype(jnp.float32).reshape(hidden_units, N_DP, slice_width)
        gate_sum = blockwise("rkd,kdf->krf", split_in, gate_blocks)
        up_sum = blockwise("rkd,kdf->krf", split_in, up_blocks)
        back_sum = blockwise("rkd,fkd->krf", split_up, down_blocks)
        hidden, grad_gate, grad_up = swiglu_grads(gate_sum, up_sum, back_sum)
        expert_out = jnp.dot(hidden, down_w, preferred_element_type=jnp.float32).astype(jnp.bfloat16)
        row_grad = (jnp.dot(grad_gate, gate_w.T, preferred_element_type=jnp.float32)
                    + jnp.dot(grad_up, up_w.T, preferred_element_type=jnp.float32)).astype(jnp.bfloat16)
        grad_down = jnp.dot(hidden.T, rows_up, preferred_element_type=jnp.float32).astype(jnp.bfloat16)
        grad_gate_w = jnp.dot(rows_in.T, grad_gate, preferred_element_type=jnp.float32).astype(jnp.bfloat16)
        grad_up_w = jnp.dot(rows_in.T, grad_up, preferred_element_type=jnp.float32).astype(jnp.bfloat16)
        return expert_out, row_grad, grad_gate_w, grad_up_w, grad_down

    expert_out, row_grad, grad_gate_w, grad_up_w, grad_down = lax.map(
        one_expert, (by_expert_in, by_expert_up, w_gate, w_up, w_down))
    out_rows = jnp.moveaxis(expert_out.reshape(expert_count, sources, slot_count, model_width), 0, 1)
    grad_back = jnp.moveaxis(row_grad.reshape(expert_count, sources, slot_count, model_width), 0, 1)
    out_float = out_rows.astype(jnp.float32)
    weighted = (gates[..., None] * out_float).reshape(-1, model_width)
    mixed = jax.ops.segment_sum(weighted, flat_rows, num_segments=tokens.shape[0]).astype(jnp.bfloat16)
    token_grad = jax.ops.segment_sum(grad_back.astype(jnp.float32).reshape(-1, model_width), flat_rows,
                                     num_segments=tokens.shape[0]).astype(jnp.bfloat16)
    gate_grad = jnp.sum(grad_rows.astype(jnp.float32) * out_float, axis=-1)
    return mixed, token_grad, gate_grad, grad_gate_w, grad_up_w, grad_down
```

```python
import functools

import jax
import jax.numpy as jnp
from jax import lax
from jax.experimental import pallas as pl
from jax.experimental.pallas import tpu as pltpu
from jax.sharding import PartitionSpec as P

MESH = pl.DeviceIdType.MESH
F32 = jnp.float32
BF16 = jnp.bfloat16


def nn(a, b):
    return lax.dot_general(a, b, (((1,), (0,)), ((), ())), preferred_element_type=F32)


def nt(a, b):
    return lax.dot_general(a, b, (((1,), (1,)), ((), ())), preferred_element_type=F32)


def tn(a, b):
    return lax.dot_general(a, b, (((0,), (0,)), ((), ())), preferred_element_type=F32)


def select_rows(rows, cols, shift):
    i = lax.broadcasted_iota(jnp.int32, (rows, cols), 0)
    c = lax.broadcasted_iota(jnp.int32, (rows, cols), 1)
    want = (i // 4) * 8 + i % 4 + shift
    return (want == c).astype(BF16)


def place_rows(rows, cols, shift):
    i = lax.broadcasted_iota(jnp.int32, (rows, cols), 1)
    c = lax.broadcasted_iota(jnp.int32, (rows, cols), 0)
    want = (i // 4) * 8 + i % 4 + shift
    return (want == c).astype(BF16)


def kernel(
    geo,
    tok, cot, idx_col, scale_col, idx_row, gate_row, wg, wu, wd,
    mixed, tgrad, ggrad, gwg, gwu, gwd,
    sbuf, rbuf, xs, ys, terms, s1, t1, s2, s3, zb_out, fin, ag, bbuf,
    a2a_send, a2a_recv, rs_send, rs_recv, z_send, z_recv, ag_send, ag_recv,
    az_send, az_recv, cb_send, cb_recv,
):
    nx, nzh, nzl, ny, nc = geo
    ne = nzl * ny * nc
    nb = nx * nzh
    n = nb * ne
    rows = ne * 8
    half = ne * 4
    tdev = tok.shape[0]
    wide = wg.shape[0]
    ff = wg.shape[1]
    hw = 3 * ff // 2
    hf = ff // 2
    dp = lax.axis_index("dp")
    ex = lax.axis_index("expert")
    me = dp * ne + ex
    x, zh = lax.div(dp, nzh), lax.rem(dp, nzh)
    core = lax.rem(ex, nc)
    yy = lax.rem(lax.div(ex, nc), ny)
    zl = lax.div(ex, nc * ny)
    zz = zh * nzl + zl

    def partner(i):
        o = lax.rem(i * 97, n)
        dc, r = lax.rem(o, nc), lax.div(o, nc)
        dx, r = lax.rem(r, nx), lax.div(r, nx)
        dy, dz = lax.rem(r, ny), lax.div(r, ny)
        px = lax.rem(x + dx, nx)
        py = lax.rem(yy + dy, ny)
        pz = lax.rem(zz + dz, nzh * nzl)
        pc = lax.rem(core + dc, nc)
        pdp = px * nzh + lax.div(pz, nzl)
        pex = (lax.rem(pz, nzl) * ny + py) * nc + pc
        return pdp, pex

    barrier = pltpu.get_barrier_semaphore()

    def greet(i, carry):
        pdp, pex = partner(i)
        pl.semaphore_signal(barrier, inc=1, device_id=(pdp, pex), device_id_type=MESH)
        return carry

    lax.fori_loop(1, n, greet, 0)

    lane = lax.broadcasted_iota(jnp.int32, (rows, tdev), 1)
    ids = idx_col[...]
    hot_t = (lane == ids).astype(BF16)
    hot_c = (lane + tdev == ids).astype(BF16)

    def gather(k, carry):
        at = pl.ds(pl.multiple_of(k * wide, 128), wide)
        got = nn(hot_t, tok[:, at]) + nn(hot_c, cot[:, at])
        got = got * scale_col[...]
        sbuf[pl.ds(k * ne, ne)] = got.reshape(ne, 8, wide).astype(BF16)
        return carry

    lax.fori_loop(0, nb, gather, 0)
    pl.semaphore_wait(barrier, n - 1)

    def exchange(src, dst, send_sem, recv_sem):
        def send(i, carry):
            pdp, pex = partner(i)
            pltpu.make_async_remote_copy(
                src_ref=src.at[pdp * ne + pex],
                dst_ref=dst.at[me],
                send_sem=send_sem,
                recv_sem=recv_sem,
                device_id=(pdp, pex),
                device_id_type=MESH,
            ).start()
            return carry

        lax.fori_loop(1, n, send, 0)
        pltpu.make_async_copy(src.at[me], dst.at[me], recv_sem).start()

    def arrived(dst, recv_sem):
        pltpu.make_async_copy(dst, dst, recv_sem).wait()

    def sent(src, send_sem):
        part = src.at[pl.ds(0, n - 1)]
        pltpu.make_async_copy(part, part, send_sem).wait()

    exchange(sbuf, rbuf, a2a_send, a2a_recv)
    arrived(rbuf, a2a_recv)

    pick_x = select_rows(half, rows, 0)
    pick_y = select_rows(half, rows, 4)

    def products(b, carry):
        z = rbuf[pl.ds(b * ne, ne)].reshape(rows, wide)
        xb = nn(pick_x, z).astype(BF16)
        yb = nn(pick_y, z).astype(BF16)
        xs[b] = xb
        ys[b] = yb
        terms[b, 0, :, :ff] = nn(xb, wg[...]).astype(BF16)
        up = nn(xb, wu[...]).astype(BF16)
        terms[b, 0, :, ff:] = up[:, :hf]
        terms[b, 1, :, :hf] = up[:, hf:]
        terms[b, 1, :, hf:] = nt(yb, wd[...]).astype(BF16)
        return carry

    lax.fori_loop(0, nb, products, 0)

    to = (lax.rem(x + 1, nx), lax.rem(x + nx - 1, nx))
    come = (to[1], to[0])
    opposite = lax.rem(x + 2, nx)
    side = (1 - zh, zh)

    def blk(q, s):
        return q * nzh + s

    def remote(src, dst, send_sem, recv_sem, pdp):
        copy = pltpu.make_async_remote_copy(
            src_ref=src, dst_ref=dst, send_sem=send_sem, recv_sem=recv_sem,
            device_id=(pdp, ex), device_id_type=MESH,
        )
        copy.start()
        return copy

    def wait_for(dst, sem):
        pltpu.make_async_copy(dst, dst, sem).wait()

    sends = []

    def rs_first(c):
        for h in (0, 1):
            sends.append(remote(terms.at[blk(opposite, side[c]), h], s1.at[c, h, 1],
                                rs_send.at[c, h, 0], rs_recv.at[c, h, 0], blk(to[h], zh)))
        for h in (0, 1):
            sends.append(remote(terms.at[blk(to[h], side[c]), 1 - h], s1.at[c, 1 - h, 0],
                                rs_send.at[c, h, 1], rs_recv.at[c, 1 - h, 1], blk(to[h], zh)))

    def rs_pass(c):
        for h in (0, 1):
            wait_for(s1.at[c, h, 1], rs_recv.at[c, h, 0])
            t1[c, h] = (terms[blk(to[h], side[c]), h].astype(F32) + s1[c, h, 1].astype(F32)).astype(BF16)
            sends.append(remote(t1.at[c, h], s2.at[c, h], rs_send.at[c, h, 2], rs_recv.at[c, h, 2],
                                blk(to[h], zh)))

    def rs_total(c, h):
        wait_for(s1.at[c, h, 0], rs_recv.at[c, h, 1])
        wait_for(s2.at[c, h], rs_recv.at[c, h, 2])
        return (terms[blk(x, side[c]), h].astype(F32) + s1[c, h, 0].astype(F32)
                + s2[c, h].astype(F32))

    zpeer = blk(x, 1 - zh)
    rs_first(0)
    rs_pass(0)
    rs_first(1)
    for h in (0, 1):
        zb_out[h] = rs_total(0, h).astype(BF16)
        sends.append(remote(zb_out.at[h], s3.at[h], z_send.at[h], z_recv.at[h], zpeer))
    rs_pass(1)
    for h in (0, 1):
        fin[h] = rs_total(1, h)
    for h in (0, 1):
        wait_for(s3.at[h], z_recv.at[h])

    step = half // 4

    def activate(i, carry):
        at = pl.ds(pl.multiple_of(i * step, step), step)
        lo = fin[0, at, :] + s3[0, at, :].astype(F32)
        hi = fin[1, at, :] + s3[1, at, :].astype(F32)
        gate = lo[:, :ff]
        up = jnp.concatenate([lo[:, ff:], hi[:, :hf]], axis=1)
        back = hi[:, hf:]
        sig = 1.0 / (1.0 + jnp.exp(-gate))
        silu = gate * sig
        hidden = (silu * up).astype(BF16)
        g_up = (back * silu).astype(BF16)
        g_gate = (back * up * sig * (1.0 + gate * (1.0 - sig))).astype(BF16)
        ag[dp, 0, at, :ff] = hidden
        ag[dp, 0, at, ff:] = g_gate[:, :hf]
        ag[dp, 1, at, :hf] = g_gate[:, hf:]
        ag[dp, 1, at, hf:] = g_up
        return carry

    lax.fori_loop(0, 4, activate, 0)

    for h in (0, 1):
        sends.append(remote(ag.at[dp, h], ag.at[dp, h], az_send.at[h], az_recv.at[h], zpeer))

    def ag_first(c, s):
        mine = blk(x, s)
        for j in (0, 1):
            for h in (0, 1):
                g = h if j == 0 else 1 - h
                sends.append(remote(ag.at[mine, g], ag.at[mine, g], ag_send.at[c, h, j],
                                    ag_recv.at[c, h, j], blk(to[h], zh)))

    def ag_pass(c, s):
        for h in (0, 1):
            got = blk(come[h], s)
            wait_for(ag.at[got, h], ag_recv.at[c, h, 0])
            sends.append(remote(ag.at[got, h], ag.at[got, h], ag_send.at[c, h, 2],
                                ag_recv.at[c, h, 2], blk(to[h], zh)))

    def ag_rest(c, s):
        for h in (0, 1):
            wait_for(ag.at[blk(come[h], s), 1 - h], ag_recv.at[c, h, 1])
            wait_for(ag.at[blk(opposite, s), h], ag_recv.at[c, h, 2])

    ag_first(0, zh)
    ag_pass(0, zh)
    for h in (0, 1):
        wait_for(ag.at[zpeer, h], az_recv.at[h])
    ag_first(1, 1 - zh)
    ag_pass(1, 1 - zh)
    ag_rest(0, zh)
    ag_rest(1, 1 - zh)

    sent(sbuf, a2a_send)
    put_x = place_rows(rows, half, 0)
    put_y = place_rows(rows, half, 4)

    def outputs(b, carry):
        out = nn(ag[b, 0, :, :ff], wd[...]).astype(BF16)
        grad = nt(ag[b, 0, :, ff:], wg[:, :hf]) + nt(ag[b, 1, :, :hf], wg[:, hf:])
        grad = (grad + nt(ag[b, 1, :, hf:], wu[...])).astype(BF16)
        both = nn(put_x, out) + nn(put_y, grad)
        sbuf[pl.ds(b * ne, ne)] = both.reshape(ne, 8, wide).astype(BF16)
        return carry

    lax.fori_loop(0, nb, outputs, 0)
    exchange(sbuf, bbuf, cb_send, cb_recv)

    all_rows = nb * half

    def grads_in(m, carry):
        at = pl.ds(pl.multiple_of(m * 128, 128), 128)
        xt = xs[:, :, at].reshape(all_rows, 128)
        gwg[at, :hf] = tn(xt, ag[:, 0, :, ff:].reshape(all_rows, hf)).astype(BF16)
        rest = tn(xt, ag[:, 1, :, :].reshape(all_rows, hw))
        gwg[at, hf:] = rest[:, :hf].astype(BF16)
        gwu[at, :] = rest[:, hf:].astype(BF16)
        return carry

    lax.fori_loop(0, wide // 128, grads_in, 0)

    def grads_down(m, carry):
        at = pl.ds(pl.multiple_of(m * 128, 128), 128)
        ht = ag[:, 0, :, at].reshape(all_rows, 128)
        gwd[at, :] = tn(ht, ys[...].reshape(all_rows, wide)).astype(BF16)
        return carry

    lax.fori_loop(0, ff // 128, grads_down, 0)

    arrived(bbuf, cb_recv)
    tline = lax.broadcasted_iota(jnp.int32, (tdev, rows), 0)
    to_out = tline == idx_row[...]
    to_grad = (tline + tdev == idx_row[...]).astype(BF16)
    weight = jnp.where(to_out, gate_row[...], 0.0)
    w_hi = weight.astype(BF16)
    w_lo = (weight - w_hi.astype(F32)).astype(BF16)

    def combine(k, prods):
        at = pl.ds(pl.multiple_of(k * wide, 128), wide)
        z = bbuf[pl.ds(k * ne, ne)].reshape(rows, wide)
        mixed[:, at] = (nn(w_hi, z) + nn(w_lo, z)).astype(BF16)
        tgrad[:, at] = nn(to_grad, z).astype(BF16)
        return prods + nt(z, cot[:, at])

    prods = lax.fori_loop(0, nb, combine, jnp.zeros((rows, tdev), F32))
    ggrad[...] = jnp.sum(jnp.where(lane == ids, prods, 0.0), axis=1, keepdims=True)
    for copy in sends:
        copy.wait_send()
    sent(sbuf, cb_send)


def body(geo, tokens, cotangent, picks, gates, w_gate, w_up, w_down):
    nx, nzh, nzl, ny, nc = geo
    ne, slots = picks.shape[1], picks.shape[2]
    nb = nx * nzh
    n = nb * ne
    tdev, model = tokens.shape
    wide, ff = w_gate.shape[1], w_gate.shape[2]
    rows, half, hw = ne * 8, ne * 4, 3 * ff // 2
    chosen, scale = picks[0], gates[0]
    idx = jnp.concatenate([chosen, chosen + tdev], axis=1)
    weight = jnp.concatenate([jnp.ones_like(scale), scale], axis=1)
    gate = jnp.concatenate([scale, scale], axis=1)
    vm = pl.BlockSpec(memory_space=pltpu.VMEM)
    outs = pl.pallas_call(
        functools.partial(kernel, geo),
        out_shape=(
            jax.ShapeDtypeStruct((tdev, model), BF16),
            jax.ShapeDtypeStruct((tdev, model), BF16),
            jax.ShapeDtypeStruct((rows, 1), F32),
            jax.ShapeDtypeStruct((wide, ff), BF16),
            jax.ShapeDtypeStruct((wide, ff), BF16),
            jax.ShapeDtypeStruct((ff, wide), BF16),
        ),
        in_specs=[vm] * 9,
        out_specs=(vm,) * 6,
        scratch_shapes=[
            pltpu.VMEM((n, 8, wide), BF16),
            pltpu.VMEM((n, 8, wide), BF16),
            pltpu.VMEM((nb, half, wide), BF16),
            pltpu.VMEM((nb, half, wide), BF16),
            pltpu.VMEM((nb, 2, half, hw), BF16),
            pltpu.VMEM((2, 2, 2, half, hw), BF16),
            pltpu.VMEM((2, 2, half, hw), BF16),
            pltpu.VMEM((2, 2, half, hw), BF16),
            pltpu.VMEM((2, half, hw), BF16),
            pltpu.VMEM((2, half, hw), BF16),
            pltpu.VMEM((2, half, hw), F32),
            pltpu.VMEM((nb, 2, half, hw), BF16),
            pltpu.VMEM((n, 8, wide), BF16),
            pltpu.SemaphoreType.DMA,
            pltpu.SemaphoreType.DMA,
            pltpu.SemaphoreType.DMA((2, 2, 3)),
            pltpu.SemaphoreType.DMA((2, 2, 3)),
            pltpu.SemaphoreType.DMA((2,)),
            pltpu.SemaphoreType.DMA((2,)),
            pltpu.SemaphoreType.DMA((2, 2, 3)),
            pltpu.SemaphoreType.DMA((2, 2, 3)),
            pltpu.SemaphoreType.DMA((2,)),
            pltpu.SemaphoreType.DMA((2,)),
            pltpu.SemaphoreType.DMA,
            pltpu.SemaphoreType.DMA,
        ],
        compiler_params=pltpu.CompilerParams(
            collective_id=0, has_side_effects=True, vmem_limit_bytes=62 * 1024 * 1024
        ),
        name="moe",
    )(
        tokens, cotangent, idx.reshape(rows, 1), weight.reshape(rows, 1),
        idx.reshape(1, rows), gate.reshape(1, rows), w_gate[0], w_up[0], w_down[0],
    )
    mixed, tgrad, ggrad, gwg, gwu, gwd = outs
    gate_grad = ggrad.reshape(ne, 8)[:, :slots].reshape(1, ne, slots)
    return (mixed, tgrad, gate_grad, gwg[None], gwu[None], gwd[None])


def solution(mesh):
    ne = mesh.shape["expert"]
    geo = (4, 2, 4, 4, 2) if ne == 32 else (4, 2, 1, 1, ne)
    return jax.shard_map(
        functools.partial(body, geo),
        mesh=mesh,
        in_specs=(
            P(("dp", "expert"), None),
            P(("dp", "expert"), None),
            P(("dp", "expert"), None, None),
            P(("dp", "expert"), None, None),
            P("expert", "dp", None),
            P("expert", "dp", None),
            P("expert", None, "dp"),
        ),
        out_specs=(
            P(("dp", "expert"), None),
            P(("dp", "expert"), None),
            P(("dp", "expert"), None, None),
            P("expert", "dp", None),
            P("expert", "dp", None),
            P("expert", None, "dp"),
        ),
        check_vma=False,
    )
```

```python
import functools

import jax
import jax.numpy as jnp
from jax import lax
from jax.experimental import pallas as pl
from jax.experimental.pallas import tpu as pltpu
from jax.sharding import PartitionSpec as P

MESH = pl.DeviceIdType.MESH
F32 = jnp.float32
BF16 = jnp.bfloat16
GREET = 5


def nn(a, b):
    return lax.dot_general(a, b, (((1,), (0,)), ((), ())), preferred_element_type=F32)


def nt(a, b):
    return lax.dot_general(a, b, (((1,), (1,)), ((), ())), preferred_element_type=F32)


def tn(a, b):
    return lax.dot_general(a, b, (((0,), (0,)), ((), ())), preferred_element_type=F32)


def select_rows(rows, cols, shift):
    i = lax.broadcasted_iota(jnp.int32, (rows, cols), 0)
    c = lax.broadcasted_iota(jnp.int32, (rows, cols), 1)
    want = (i // 4) * 8 + i % 4 + shift
    return (want == c).astype(BF16)


def place_rows(rows, cols, shift):
    i = lax.broadcasted_iota(jnp.int32, (rows, cols), 1)
    c = lax.broadcasted_iota(jnp.int32, (rows, cols), 0)
    want = (i // 4) * 8 + i % 4 + shift
    return (want == c).astype(BF16)


def kernel(
    geo,
    tok, cot, pick_row, gate_row, wg, wu, wd,
    mixed, tgrad, ggrad, gwg, gwu, gwd,
    sbuf, rbuf, xs, ys, terms, s1, t1, s2, s3, zb_out, fin, ag, bbuf,
    a2a_send, a2a_recv, rs_send, rs_recv, z_send, z_recv, ag_send, ag_recv,
    az_send, az_recv, cb_send, cb_recv,
):
    nx, nzh, nzl, ny, nc = geo
    ne = nzl * ny * nc
    nb = nx * nzh
    n = nb * ne
    nz = nzh * nzl
    per = nz * ny * nc
    rows = ne * 8
    half = ne * 4
    tdev = tok.shape[0]
    wide = wg.shape[0]
    ff = wg.shape[1]
    hw = 3 * ff // 2
    hf = ff // 2
    dp = lax.axis_index("dp")
    ex = lax.axis_index("expert")
    me = dp * ne + ex
    x, zh = lax.div(dp, nzh), lax.rem(dp, nzh)
    core = lax.rem(ex, nc)
    yy = lax.rem(lax.div(ex, nc), ny)
    zl = lax.div(ex, nc * ny)
    zz = zh * nzl + zl

    barrier = pltpu.get_barrier_semaphore()

    def greet(i, carry):
        other = lax.rem(me + i, n)
        pl.semaphore_signal(barrier, inc=1, device_id=other, device_id_type=pl.DeviceIdType.LOGICAL)
        return carry

    lax.fori_loop(1, n, greet, 0, unroll=GREET)

    pick_x = select_rows(half, rows, 0)
    pick_y = select_rows(half, rows, 4)
    put_x = place_rows(rows, half, 0)
    put_y = place_rows(rows, half, 4)
    eye = lax.broadcasted_iota(jnp.int32, (half, half), 0) == lax.broadcasted_iota(
        jnp.int32, (half, half), 1
    )
    pick_col = jnp.sum(jnp.where(eye, pick_row[...], 0), axis=1, keepdims=True)
    gate_col = jnp.sum(jnp.where(eye, gate_row[...], 0.0), axis=1, keepdims=True)
    hot = (lax.broadcasted_iota(jnp.int32, (half, tdev), 1) == pick_col).astype(BF16)

    def gather(k, carry):
        at = pl.ds(pl.multiple_of(k * wide, 128), wide)
        token_rows = nn(hot, tok[:, at]).astype(BF16)
        grad_rows = (nn(hot, cot[:, at]) * gate_col).astype(BF16)
        both = nn(put_x, token_rows) + nn(put_y, grad_rows)
        sbuf[pl.ds(k * ne, ne)] = both.reshape(ne, 8, wide).astype(BF16)
        return carry

    lax.fori_loop(0, nb, gather, 0)
    pl.semaphore_wait(barrier, n - 1)

    def dispatch(ways, first):
        def send(i, carry):
            dx = ways[0]
            if len(ways) == 2:
                dx = ways[0] + (ways[1] - ways[0]) * lax.rem(i, 2)
            o = lax.rem(lax.div(i, len(ways)) * 37, per)
            dc, r = lax.rem(o, nc), lax.div(o, nc)
            dz, dy = lax.rem(r, nz), lax.div(r, nz)
            pz = lax.rem(zz + dz, nz)
            pdp = lax.rem(x + dx, nx) * nzh + lax.div(pz, nzl)
            pex = (lax.rem(pz, nzl) * ny + lax.rem(yy + dy, ny)) * nc + lax.rem(core + dc, nc)
            pltpu.make_async_remote_copy(
                src_ref=sbuf.at[pdp * ne + pex], dst_ref=rbuf.at[me],
                send_sem=a2a_send, recv_sem=a2a_recv.at[dp],
                device_id=(pdp, pex), device_id_type=MESH,
            ).start()
            return carry

        lax.fori_loop(first, per * len(ways), send, 0)

    dispatch((2,), 0)
    dispatch((1, 3), 0)
    dispatch((0,), 1)
    pltpu.make_async_copy(sbuf.at[me], rbuf.at[me], a2a_recv.at[dp]).start()

    def sent(src, send_sem):
        part = src.at[pl.ds(0, n - 1)]
        pltpu.make_async_copy(part, part, send_sem).wait()

    def products(b):
        part = rbuf.at[pl.ds(b * ne, ne)]
        pltpu.make_async_copy(part, part, a2a_recv.at[b]).wait()
        z = rbuf[pl.ds(b * ne, ne)].reshape(rows, wide)
        xb = nn(pick_x, z).astype(BF16)
        yb = nn(pick_y, z).astype(BF16)
        xs[b] = xb
        ys[b] = yb
        terms[b, 0, :, :ff] = nn(xb, wg[...]).astype(BF16)
        up = nn(xb, wu[...]).astype(BF16)
        terms[b, 0, :, ff:] = up[:, :hf]
        terms[b, 1, :, :hf] = up[:, hf:]
        terms[b, 1, :, hf:] = nt(yb, wd[...]).astype(BF16)

    to = (lax.rem(x + 1, nx), lax.rem(x + nx - 1, nx))
    come = (to[1], to[0])
    opposite = lax.rem(x + 2, nx)
    side = (1 - zh, zh)

    def blk(q, s):
        return q * nzh + s

    def remote(src, dst, send_sem, recv_sem, pdp):
        copy = pltpu.make_async_remote_copy(
            src_ref=src, dst_ref=dst, send_sem=send_sem, recv_sem=recv_sem,
            device_id=(pdp, ex), device_id_type=MESH,
        )
        copy.start()
        return copy

    def wait_for(dst, sem):
        pltpu.make_async_copy(dst, dst, sem).wait()

    sends = []

    def rs_first(c):
        for h in (0, 1):
            sends.append(remote(terms.at[blk(opposite, side[c]), h], s1.at[c, h, 1],
                                rs_send.at[c, h, 0], rs_recv.at[c, h, 0], blk(to[h], zh)))

    def rs_pass(c):
        for h in (0, 1):
            sends.append(remote(terms.at[blk(to[h], side[c]), 1 - h], s1.at[c, 1 - h, 0],
                                rs_send.at[c, h, 1], rs_recv.at[c, 1 - h, 1], blk(to[h], zh)))
        for h in (0, 1):
            wait_for(s1.at[c, h, 1], rs_recv.at[c, h, 0])
            t1[c, h] = (terms[blk(to[h], side[c]), h].astype(F32) + s1[c, h, 1].astype(F32)).astype(BF16)
            sends.append(remote(t1.at[c, h], s2.at[c, h], rs_send.at[c, h, 2], rs_recv.at[c, h, 2],
                                blk(to[h], zh)))

    def rs_total(c, h):
        wait_for(s1.at[c, h, 0], rs_recv.at[c, h, 1])
        wait_for(s2.at[c, h], rs_recv.at[c, h, 2])
        return (terms[blk(x, side[c]), h].astype(F32) + s1[c, h, 0].astype(F32)
                + s2[c, h].astype(F32))

    def products_of(first, gap, count):
        def one(i, carry):
            products(blk(lax.rem(first + gap * lax.div(i, nzh), nx), lax.rem(i, nzh)))
            return carry

        lax.fori_loop(0, count * nzh, one, 0)

    zpeer = blk(x, 1 - zh)
    products_of(opposite, 0, 1)
    rs_first(0)
    rs_first(1)
    products_of(x + 1, 2, 2)
    rs_pass(0)
    rs_pass(1)
    products_of(x, 0, 1)
    for h in (0, 1):
        zb_out[h] = rs_total(0, h).astype(BF16)
        sends.append(remote(zb_out.at[h], s3.at[h], z_send.at[h], z_recv.at[h], zpeer))
    for h in (0, 1):
        fin[h] = rs_total(1, h)
    sent(sbuf, a2a_send)
    for h in (0, 1):
        wait_for(s3.at[h], z_recv.at[h])

    step = half // 4

    def activate(i, carry):
        at = pl.ds(pl.multiple_of(i * step, step), step)
        lo = fin[0, at, :] + s3[0, at, :].astype(F32)
        hi = fin[1, at, :] + s3[1, at, :].astype(F32)
        gate = lo[:, :ff]
        up = jnp.concatenate([lo[:, ff:], hi[:, :hf]], axis=1)
        back = hi[:, hf:]
        sig = 1.0 / (1.0 + jnp.exp(-gate))
        silu = gate * sig
        hidden = (silu * up).astype(BF16)
        g_up = (back * silu).astype(BF16)
        g_gate = (back * up * sig * (1.0 + gate * (1.0 - sig))).astype(BF16)
        ag[dp, 0, at, :ff] = hidden
        ag[dp, 0, at, ff:] = g_gate[:, :hf]
        ag[dp, 1, at, :hf] = g_gate[:, hf:]
        ag[dp, 1, at, hf:] = g_up
        return carry

    lax.fori_loop(0, 4, activate, 0)

    def ag_first(c, s, g):
        mine = blk(x, s)
        for h in (g, 1 - g):
            j = 0 if g == h else 1
            sends.append(remote(ag.at[mine, g], ag.at[mine, g], ag_send.at[c, h, j],
                                ag_recv.at[c, h, j], blk(to[h], zh)))

    def ag_pass(c, s):
        for h in (0, 1):
            got = blk(come[h], s)
            wait_for(ag.at[got, h], ag_recv.at[c, h, 0])
            sends.append(remote(ag.at[got, h], ag.at[got, h], ag_send.at[c, h, 2],
                                ag_recv.at[c, h, 2], blk(to[h], zh)))

    def outputs(b, first):
        out = nn(ag[b, 0, :, :ff], wd[...]).astype(BF16)
        grad = nt(ag[b, 0, :, ff:], wg[:, :hf]) + nt(ag[b, 1, :, :hf], wg[:, hf:])
        grad = (grad + nt(ag[b, 1, :, hf:], wu[...])).astype(BF16)
        both = nn(put_x, out) + nn(put_y, grad)
        sbuf[pl.ds(b * ne, ne)] = both.reshape(ne, 8, wide).astype(BF16)

        def send(i, carry):
            o = lax.rem(i * 13, ne)
            dc, r = lax.rem(o, nc), lax.div(o, nc)
            dy, dz = lax.rem(r, ny), lax.div(r, ny)
            pex = (lax.rem(zl + dz, nzl) * ny + lax.rem(yy + dy, ny)) * nc + lax.rem(core + dc, nc)
            pltpu.make_async_remote_copy(
                src_ref=sbuf.at[b * ne + pex], dst_ref=bbuf.at[me],
                send_sem=cb_send, recv_sem=cb_recv.at[dp],
                device_id=(b, pex), device_id_type=MESH,
            ).start()
            return carry

        lax.fori_loop(first, ne, send, 0)

    def outputs_beside(s):
        def one(i, carry):
            outputs(blk(lax.rem(x + 1 + 2 * i, nx), s), 0)
            return carry

        lax.fori_loop(0, 2, one, 0)

    def ag_side(c, s):
        for h in (0, 1):
            wait_for(ag.at[blk(come[h], s), 1 - h], ag_recv.at[c, h, 1])

    def ag_far(c, s):
        for h in (0, 1):
            wait_for(ag.at[blk(opposite, s), h], ag_recv.at[c, h, 2])

    for h in (0, 1):
        sends.append(remote(ag.at[dp, h], ag.at[dp, h], az_send.at[h], az_recv.at[h], zpeer))
    ag_first(0, zh, 0)
    ag_first(0, zh, 1)
    outputs(dp, 1)
    pltpu.make_async_copy(sbuf.at[me], bbuf.at[me], cb_recv.at[dp]).start()
    ag_pass(0, zh)
    ag_side(0, zh)
    outputs_beside(zh)
    wait_for(ag.at[zpeer, 0], az_recv.at[0])
    ag_first(1, 1 - zh, 0)
    ag_far(0, zh)
    outputs(blk(opposite, zh), 0)
    wait_for(ag.at[zpeer, 1], az_recv.at[1])
    ag_first(1, 1 - zh, 1)
    outputs(zpeer, 0)
    ag_pass(1, 1 - zh)
    ag_side(1, 1 - zh)
    outputs_beside(1 - zh)
    ag_far(1, 1 - zh)
    outputs(blk(opposite, 1 - zh), 0)

    all_rows = nb * half

    def grads_in(m, carry):
        at = pl.ds(pl.multiple_of(m * 128, 128), 128)
        xt = xs[:, :, at].reshape(all_rows, 128)
        gwg[at, :hf] = tn(xt, ag[:, 0, :, ff:].reshape(all_rows, hf)).astype(BF16)
        rest = tn(xt, ag[:, 1, :, :].reshape(all_rows, hw))
        gwg[at, hf:] = rest[:, :hf].astype(BF16)
        gwu[at, :] = rest[:, hf:].astype(BF16)
        return carry

    lax.fori_loop(0, wide // 128, grads_in, 0)

    def grads_down(m, carry):
        at = pl.ds(pl.multiple_of(m * 128, 128), 128)
        ht = ag[:, 0, :, at].reshape(all_rows, 128)
        gwd[at, :] = tn(ht, ys[...].reshape(all_rows, wide)).astype(BF16)
        return carry

    lax.fori_loop(0, ff // 128, grads_down, 0)

    here = lax.broadcasted_iota(jnp.int32, (tdev, half), 0) == pick_row[...]
    to_grad = nn(here.astype(BF16), pick_y).astype(BF16)
    weight = jnp.where(here, gate_row[...], 0.0)
    w_hi = weight.astype(BF16)
    w_lo = nn((weight - w_hi.astype(F32)).astype(BF16), pick_x).astype(BF16)
    w_hi = nn(w_hi, pick_x).astype(BF16)

    def combine(i, prods):
        j = lax.rem(i, nx)
        j = j + lax.div(j, 2) * (1 - 2 * lax.rem(j, 2))
        s = lax.rem(zh + lax.div(i, nx), nzh)
        k = blk(lax.rem(x + j, nx), s)
        part = bbuf.at[pl.ds(k * ne, ne)]
        pltpu.make_async_copy(part, part, cb_recv.at[k]).wait()
        at = pl.ds(pl.multiple_of(k * wide, 128), wide)
        z = bbuf[pl.ds(k * ne, ne)].reshape(rows, wide)
        mixed[:, at] = (nn(w_hi, z) + nn(w_lo, z)).astype(BF16)
        tgrad[:, at] = nn(to_grad, z).astype(BF16)
        return prods + nt(cot[:, at], nn(pick_x, z).astype(BF16))

    prods = lax.fori_loop(0, nb, combine, jnp.zeros((tdev, half), F32))
    ggrad[...] = jnp.sum(jnp.where(here, prods, 0.0), axis=0, keepdims=True)
    for copy in sends:
        copy.wait_send()
    sent(sbuf, cb_send)


def body(geo, tokens, cotangent, picks, gates, w_gate, w_up, w_down):
    nx, nzh, nzl, ny, nc = geo
    ne, slots = picks.shape[1], picks.shape[2]
    nb = nx * nzh
    n = nb * ne
    tdev, model = tokens.shape
    wide, ff = w_gate.shape[1], w_gate.shape[2]
    half, hw = ne * 4, 3 * ff // 2
    vm = pl.BlockSpec(memory_space=pltpu.VMEM)
    outs = pl.pallas_call(
        functools.partial(kernel, geo),
        out_shape=(
            jax.ShapeDtypeStruct((tdev, model), BF16),
            jax.ShapeDtypeStruct((tdev, model), BF16),
            jax.ShapeDtypeStruct((1, half), F32),
            jax.ShapeDtypeStruct((wide, ff), BF16),
            jax.ShapeDtypeStruct((wide, ff), BF16),
            jax.ShapeDtypeStruct((ff, wide), BF16),
        ),
        in_specs=[vm] * 7,
        out_specs=(vm,) * 6,
        scratch_shapes=[
            pltpu.VMEM((n, 8, wide), BF16),
            pltpu.VMEM((n, 8, wide), BF16),
            pltpu.VMEM((nb, half, wide), BF16),
            pltpu.VMEM((nb, half, wide), BF16),
            pltpu.VMEM((nb, 2, half, hw), BF16),
            pltpu.VMEM((2, 2, 2, half, hw), BF16),
            pltpu.VMEM((2, 2, half, hw), BF16),
            pltpu.VMEM((2, 2, half, hw), BF16),
            pltpu.VMEM((2, half, hw), BF16),
            pltpu.VMEM((2, half, hw), BF16),
            pltpu.VMEM((2, half, hw), F32),
            pltpu.VMEM((nb, 2, half, hw), BF16),
            pltpu.VMEM((n, 8, wide), BF16),
            pltpu.SemaphoreType.DMA,
            pltpu.SemaphoreType.DMA((nb,)),
            pltpu.SemaphoreType.DMA((2, 2, 3)),
            pltpu.SemaphoreType.DMA((2, 2, 3)),
            pltpu.SemaphoreType.DMA((2,)),
            pltpu.SemaphoreType.DMA((2,)),
            pltpu.SemaphoreType.DMA((2, 2, 3)),
            pltpu.SemaphoreType.DMA((2, 2, 3)),
            pltpu.SemaphoreType.DMA((2,)),
            pltpu.SemaphoreType.DMA((2,)),
            pltpu.SemaphoreType.DMA,
            pltpu.SemaphoreType.DMA((nb,)),
        ],
        compiler_params=pltpu.CompilerParams(
            collective_id=0, has_side_effects=True, vmem_limit_bytes=62 * 1024 * 1024
        ),
        name="moe",
    )(
        tokens, cotangent, picks.reshape(1, half), gates.reshape(1, half),
        w_gate[0], w_up[0], w_down[0],
    )
    mixed, tgrad, ggrad, gwg, gwu, gwd = outs
    gate_grad = ggrad.reshape(1, ne, slots)
    return (mixed, tgrad, gate_grad, gwg[None], gwu[None], gwd[None])


def solution(mesh):
    ne = mesh.shape["expert"]
    geo = (4, 2, 4, 4, 2) if ne == 32 else (4, 2, 1, 1, ne)
    return jax.shard_map(
        functools.partial(body, geo),
        mesh=mesh,
        in_specs=(
            P(("dp", "expert"), None),
            P(("dp", "expert"), None),
            P(("dp", "expert"), None, None),
            P(("dp", "expert"), None, None),
            P("expert", "dp", None),
            P("expert", "dp", None),
            P("expert", None, "dp"),
        ),
        out_specs=(
            P(("dp", "expert"), None),
            P(("dp", "expert"), None),
            P(("dp", "expert"), None, None),
            P("expert", "dp", None),
            P("expert", "dp", None),
            P("expert", None, "dp"),
        ),
        check_vma=False,
    )
```

```python
import functools

import jax
import jax.numpy as jnp
from jax import lax
from jax.experimental import pallas as pl
from jax.experimental.pallas import tpu as pltpu
from jax.sharding import PartitionSpec as P

MESH = pl.DeviceIdType.MESH
F32 = jnp.float32
BF16 = jnp.bfloat16
GREET = 5


def nn(a, b):
    return lax.dot_general(a, b, (((1,), (0,)), ((), ())), preferred_element_type=F32)


def nt(a, b):
    return lax.dot_general(a, b, (((1,), (1,)), ((), ())), preferred_element_type=F32)


def tn(a, b):
    return lax.dot_general(a, b, (((0,), (0,)), ((), ())), preferred_element_type=F32)


def select_rows(rows, cols, shift):
    i = lax.broadcasted_iota(jnp.int32, (rows, cols), 0)
    c = lax.broadcasted_iota(jnp.int32, (rows, cols), 1)
    want = (i // 4) * 8 + i % 4 + shift
    return (want == c).astype(BF16)


def place_rows(rows, cols, shift):
    i = lax.broadcasted_iota(jnp.int32, (rows, cols), 1)
    c = lax.broadcasted_iota(jnp.int32, (rows, cols), 0)
    want = (i // 4) * 8 + i % 4 + shift
    return (want == c).astype(BF16)


def kernel(
    geo,
    tok_in, cot_in, pick_in, gate_in, wg_in, wu_in, wd_in,
    mixed_out, tgrad_out, ggrad, gwg_out, gwu_out, gwd_out,
    tok, cot, wg, wu, wd, mixed, tgrad, gwg, gwu, gwd,
    sbuf, rbuf, xs, ys, terms, s1, t1, s2, s3, zb_out, ag, bbuf,
    in_sem, out_sem, a2a_send, a2a_recv, rs_send, rs_recv, z_send, z_recv, ag_send, ag_recv,
    cb_send, cb_recv,
):
    nx, nzh, nzl, ny, nc = geo
    ne = nzl * ny * nc
    nb = nx * nzh
    n = nb * ne
    nz = nzh * nzl
    per = nz * ny * nc
    rows = ne * 8
    half = ne * 4
    tdev = tok.shape[0]
    wide = wg.shape[0]
    ff = wg.shape[1]
    hw = 3 * ff // 2
    hf = ff // 2
    dp = lax.axis_index("dp")
    ex = lax.axis_index("expert")
    me = dp * ne + ex
    x, zh = lax.div(dp, nzh), lax.rem(dp, nzh)
    core = lax.rem(ex, nc)
    yy = lax.rem(lax.div(ex, nc), ny)
    zl = lax.div(ex, nc * ny)
    zz = zh * nzl + zl

    loads = [
        pltpu.make_async_copy(src, dst, in_sem.at[i])
        for i, (src, dst) in enumerate(
            ((tok_in, tok), (cot_in, cot), (wg_in, wg), (wu_in, wu), (wd_in, wd))
        )
    ]
    barrier = pltpu.get_barrier_semaphore()
    for load in loads:
        load.start()

    def greet(i, carry):
        other = lax.rem(me + i, n)
        pl.semaphore_signal(barrier, inc=1, device_id=other, device_id_type=pl.DeviceIdType.LOGICAL)
        return carry

    lax.fori_loop(1, n, greet, 0, unroll=GREET)

    pick_x = select_rows(half, rows, 0)
    pick_y = select_rows(half, rows, 4)
    put_x = place_rows(rows, half, 0)
    put_y = place_rows(rows, half, 4)
    eye = lax.broadcasted_iota(jnp.int32, (half, half), 0) == lax.broadcasted_iota(
        jnp.int32, (half, half), 1
    )
    slot = lax.broadcasted_iota(jnp.int32, (4, half), 0) == lax.rem(
        lax.broadcasted_iota(jnp.int32, (4, half), 1), 4
    )
    spread = (
        lax.broadcasted_iota(jnp.int32, (ne, half), 0)
        == lax.div(lax.broadcasted_iota(jnp.int32, (ne, half), 1), 4)
    ).astype(BF16)

    def pieces(v):
        top = v.astype(BF16)
        rest = v - top.astype(F32)
        mid = rest.astype(BF16)
        return top, mid, (rest - mid.astype(F32)).astype(BF16)

    def in_row(v):
        top, mid, low = pieces(v)
        wide_v = nn(top, spread) + nn(mid, spread) + nn(low, spread)
        return jnp.sum(jnp.where(slot, wide_v, 0.0), axis=0, keepdims=True)

    pick_row = in_row(pick_in[...].astype(F32)).astype(jnp.int32)
    gate_row = in_row(gate_in[...])
    pick_col = jnp.sum(jnp.where(eye, pick_row, 0), axis=1, keepdims=True)
    gate_col = jnp.sum(jnp.where(eye, gate_row, 0.0), axis=1, keepdims=True)
    hot = (lax.broadcasted_iota(jnp.int32, (half, tdev), 1) == pick_col).astype(BF16)

    def gather(k, carry):
        at = pl.ds(pl.multiple_of(k * wide, 128), wide)
        token_rows = nn(hot, tok[:, at]).astype(BF16)
        grad_rows = (nn(hot, cot[:, at]) * gate_col).astype(BF16)
        both = nn(put_x, token_rows) + nn(put_y, grad_rows)
        sbuf[pl.ds(k * ne, ne)] = both.reshape(ne, 8, wide).astype(BF16)
        return carry

    loads[0].wait()
    loads[1].wait()
    lax.fori_loop(0, nb, gather, 0)
    pl.semaphore_wait(barrier, n - 1)

    def dispatch(ways, first):
        def send(i, carry):
            dx = ways[0]
            if len(ways) == 2:
                dx = ways[0] + (ways[1] - ways[0]) * lax.rem(i, 2)
            o = lax.rem(lax.div(i, len(ways)) * 37, per)
            dc, r = lax.rem(o, nc), lax.div(o, nc)
            dz, dy = lax.rem(r, nz), lax.div(r, nz)
            pz = lax.rem(zz + dz, nz)
            pdp = lax.rem(x + dx, nx) * nzh + lax.div(pz, nzl)
            pex = (lax.rem(pz, nzl) * ny + lax.rem(yy + dy, ny)) * nc + lax.rem(core + dc, nc)
            pltpu.make_async_remote_copy(
                src_ref=sbuf.at[pdp * ne + pex], dst_ref=rbuf.at[me],
                send_sem=a2a_send, recv_sem=a2a_recv.at[dp],
                device_id=(pdp, pex), device_id_type=MESH,
            ).start()
            return carry

        lax.fori_loop(first, per * len(ways), send, 0)

    dispatch((2,), 0)
    dispatch((1, 3), 0)
    dispatch((0,), 1)
    pltpu.make_async_copy(sbuf.at[me], rbuf.at[me], a2a_recv.at[dp]).start()

    def sent(src, send_sem):
        part = src.at[pl.ds(0, n - 1)]
        pltpu.make_async_copy(part, part, send_sem).wait()

    def products(b):
        part = rbuf.at[pl.ds(b * ne, ne)]
        pltpu.make_async_copy(part, part, a2a_recv.at[b]).wait()
        z = rbuf[pl.ds(b * ne, ne)].reshape(rows, wide)
        xb = nn(pick_x, z).astype(BF16)
        yb = nn(pick_y, z).astype(BF16)
        xs[b] = xb
        ys[b] = yb
        terms[b, 0, :, :ff] = nn(xb, wg[...]).astype(BF16)
        up = nn(xb, wu[...]).astype(BF16)
        terms[b, 0, :, ff:] = up[:, :hf]
        terms[b, 1, :, :hf] = up[:, hf:]
        terms[b, 1, :, hf:] = nt(yb, wd[...]).astype(BF16)

    to = (lax.rem(x + 1, nx), lax.rem(x + nx - 1, nx))
    come = (to[1], to[0])
    opposite = lax.rem(x + 2, nx)
    side = (zh, 1 - zh)

    def blk(q, s):
        return q * nzh + s

    def remote(src, dst, send_sem, recv_sem, pdp):
        copy = pltpu.make_async_remote_copy(
            src_ref=src, dst_ref=dst, send_sem=send_sem, recv_sem=recv_sem,
            device_id=(pdp, ex), device_id_type=MESH,
        )
        copy.start()
        return copy

    def wait_for(dst, sem):
        pltpu.make_async_copy(dst, dst, sem).wait()

    sends = []

    def rs_first(c):
        for h in (0, 1):
            sends.append(remote(terms.at[blk(opposite, side[c]), h], s1.at[c, h, 1],
                                rs_send.at[c, h, 0], rs_recv.at[c, h, 0], blk(to[h], zh)))

    def rs_pass(c):
        for h in (0, 1):
            sends.append(remote(terms.at[blk(to[h], side[c]), 1 - h], s1.at[c, 1 - h, 0],
                                rs_send.at[c, h, 1], rs_recv.at[c, 1 - h, 1], blk(to[h], zh)))
        for h in (0, 1):
            wait_for(s1.at[c, h, 1], rs_recv.at[c, h, 0])
            t1[c, h] = (terms[blk(to[h], side[c]), h].astype(F32) + s1[c, h, 1].astype(F32)).astype(BF16)
            sends.append(remote(t1.at[c, h], s2.at[c, h], rs_send.at[c, h, 2], rs_recv.at[c, h, 2],
                                blk(to[h], zh)))

    def rs_total(c, h):
        wait_for(s1.at[c, h, 0], rs_recv.at[c, h, 1])
        wait_for(s2.at[c, h], rs_recv.at[c, h, 2])
        return (terms[blk(x, side[c]), h].astype(F32) + s1[c, h, 0].astype(F32)
                + s2[c, h].astype(F32))

    def products_of(first, gap, count):
        def one(i, carry):
            products(blk(lax.rem(first + gap * lax.div(i, nzh), nx), lax.rem(i, nzh)))
            return carry

        lax.fori_loop(0, count * nzh, one, 0)

    zpeer = blk(x, 1 - zh)
    for load in loads[2:]:
        load.wait()
    products_of(opposite, 0, 1)
    rs_first(0)
    rs_first(1)
    products_of(x + 1, 2, 2)
    rs_pass(0)
    rs_pass(1)
    products_of(x, 0, 1)
    for c in (0, 1):
        for h in (0, 1):
            zb_out[c, h] = rs_total(c, h).astype(BF16)
            sends.append(remote(zb_out.at[c, h], s3.at[c, h], z_send.at[c, h], z_recv.at[c, h], zpeer))
    sent(sbuf, a2a_send)

    step = half // 4

    def activate(b, c):
        for h in (0, 1):
            wait_for(s3.at[c, h], z_recv.at[c, h])

        def part(i, carry):
            at = pl.ds(pl.multiple_of(i * step, step), step)
            lo = zb_out[1 - c, 0, at, :].astype(F32) + s3[c, 0, at, :].astype(F32)
            hi = zb_out[1 - c, 1, at, :].astype(F32) + s3[c, 1, at, :].astype(F32)
            gate = lo[:, :ff]
            up = jnp.concatenate([lo[:, ff:], hi[:, :hf]], axis=1)
            back = hi[:, hf:]
            sig = 1.0 / (1.0 + jnp.exp(-gate))
            silu = gate * sig
            hidden = (silu * up).astype(BF16)
            g_up = (back * silu).astype(BF16)
            g_gate = (back * up * sig * (1.0 + gate * (1.0 - sig))).astype(BF16)
            ag[b, 0, at, :ff] = hidden
            ag[b, 0, at, ff:] = g_gate[:, :hf]
            ag[b, 1, at, :hf] = g_gate[:, hf:]
            ag[b, 1, at, hf:] = g_up
            return carry

        lax.fori_loop(0, 4, part, 0)

    def ag_first(c, s, g):
        mine = blk(x, s)
        for h in (g, 1 - g):
            j = 0 if g == h else 1
            sends.append(remote(ag.at[mine, g], ag.at[mine, g], ag_send.at[c, h, j],
                                ag_recv.at[c, h, j], blk(to[h], zh)))

    def ag_pass(c, s):
        for h in (0, 1):
            got = blk(come[h], s)
            wait_for(ag.at[got, h], ag_recv.at[c, h, 0])
            sends.append(remote(ag.at[got, h], ag.at[got, h], ag_send.at[c, h, 2],
                                ag_recv.at[c, h, 2], blk(to[h], zh)))

    def outputs(b, first):
        out = nn(ag[b, 0, :, :ff], wd[...]).astype(BF16)
        grad = nt(ag[b, 0, :, ff:], wg[:, :hf]) + nt(ag[b, 1, :, :hf], wg[:, hf:])
        grad = (grad + nt(ag[b, 1, :, hf:], wu[...])).astype(BF16)
        both = nn(put_x, out) + nn(put_y, grad)
        sbuf[pl.ds(b * ne, ne)] = both.reshape(ne, 8, wide).astype(BF16)

        def send(i, carry):
            o = lax.rem(i * 13, ne)
            dc, r = lax.rem(o, nc), lax.div(o, nc)
            dy, dz = lax.rem(r, ny), lax.div(r, ny)
            pex = (lax.rem(zl + dz, nzl) * ny + lax.rem(yy + dy, ny)) * nc + lax.rem(core + dc, nc)
            pltpu.make_async_remote_copy(
                src_ref=sbuf.at[b * ne + pex], dst_ref=bbuf.at[me],
                send_sem=cb_send, recv_sem=cb_recv.at[dp],
                device_id=(b, pex), device_id_type=MESH,
            ).start()
            return carry

        lax.fori_loop(first, ne, send, 0)

    def outputs_beside(s):
        def one(i, carry):
            outputs(blk(lax.rem(x + 1 + 2 * i, nx), s), 0)
            return carry

        lax.fori_loop(0, 2, one, 0)

    def ag_side(c, s):
        for h in (0, 1):
            wait_for(ag.at[blk(come[h], s), 1 - h], ag_recv.at[c, h, 1])

    def ag_far(c, s):
        for h in (0, 1):
            wait_for(ag.at[blk(opposite, s), h], ag_recv.at[c, h, 2])

    activate(zpeer, 0)
    ag_first(0, 1 - zh, 0)
    ag_first(0, 1 - zh, 1)
    outputs(zpeer, 0)
    ag_pass(0, 1 - zh)
    ag_side(0, 1 - zh)
    outputs_beside(1 - zh)
    ag_far(0, 1 - zh)
    outputs(blk(opposite, 1 - zh), 0)
    activate(dp, 1)
    ag_first(1, zh, 0)
    ag_first(1, zh, 1)
    outputs(dp, 1)
    pltpu.make_async_copy(sbuf.at[me], bbuf.at[me], cb_recv.at[dp]).start()
    ag_pass(1, zh)
    ag_side(1, zh)
    outputs_beside(zh)
    ag_far(1, zh)
    outputs(blk(opposite, zh), 0)

    all_rows = nb * half

    def grads_in(m, carry):
        at = pl.ds(pl.multiple_of(m * 128, 128), 128)
        xt = xs[:, :, at].reshape(all_rows, 128)
        gwg[at, :hf] = tn(xt, ag[:, 0, :, ff:].reshape(all_rows, hf)).astype(BF16)
        rest = tn(xt, ag[:, 1, :, :].reshape(all_rows, hw))
        gwg[at, hf:] = rest[:, :hf].astype(BF16)
        gwu[at, :] = rest[:, hf:].astype(BF16)
        return carry

    lax.fori_loop(0, wide // 128, grads_in, 0)

    def grads_down(m, carry):
        at = pl.ds(pl.multiple_of(m * 128, 128), 128)
        ht = ag[:, 0, :, at].reshape(all_rows, 128)
        gwd[at, :] = tn(ht, ys[...].reshape(all_rows, wide)).astype(BF16)
        return carry

    lax.fori_loop(0, ff // 128, grads_down, 0)

    stores = [
        pltpu.make_async_copy(src, dst, out_sem.at[i])
        for i, (src, dst) in enumerate(((gwg, gwg_out), (gwu, gwu_out), (gwd, gwd_out)))
    ]
    for store in stores:
        store.start()

    here = lax.broadcasted_iota(jnp.int32, (tdev, half), 0) == pick_row
    to_grad = nn(here.astype(BF16), pick_y).astype(BF16)
    weight = jnp.where(here, gate_row, 0.0)
    w_hi = weight.astype(BF16)
    w_lo = nn((weight - w_hi.astype(F32)).astype(BF16), pick_x).astype(BF16)
    w_hi = nn(w_hi, pick_x).astype(BF16)

    def combine(i, prods):
        j = lax.rem(i, nx)
        j = j + lax.div(j, 2) * (1 - 2 * lax.rem(j, 2))
        s = lax.rem(zh + lax.div(i, nx), nzh)
        k = blk(lax.rem(x + j, nx), s)
        part = bbuf.at[pl.ds(k * ne, ne)]
        pltpu.make_async_copy(part, part, cb_recv.at[k]).wait()
        at = pl.ds(pl.multiple_of(k * wide, 128), wide)
        z = bbuf[pl.ds(k * ne, ne)].reshape(rows, wide)
        mixed[:, at] = (nn(w_hi, z) + nn(w_lo, z)).astype(BF16)
        tgrad[:, at] = nn(to_grad, z).astype(BF16)
        pltpu.make_async_copy(mixed.at[:, at], mixed_out.at[:, at], out_sem.at[3]).start()
        pltpu.make_async_copy(tgrad.at[:, at], tgrad_out.at[:, at], out_sem.at[4]).start()
        return prods + nt(cot[:, at], nn(pick_x, z).astype(BF16))

    prods = lax.fori_loop(0, nb, combine, jnp.zeros((tdev, half), F32))
    total = jnp.sum(jnp.where(here, prods, 0.0), axis=0, keepdims=True)
    top, mid, low = pieces(jnp.where(slot, total, 0.0))
    ggrad[...] = nt(top, spread) + nt(mid, spread) + nt(low, spread)
    for store in stores:
        store.wait()
    pltpu.make_async_copy(mixed, mixed_out, out_sem.at[3]).wait()
    pltpu.make_async_copy(tgrad, tgrad_out, out_sem.at[4]).wait()
    for copy in sends:
        copy.wait_send()
    sent(sbuf, cb_send)


def hand_on(*refs):
    count = (len(refs) - 2) // 3
    ins, outs, bufs = refs[:count], refs[count : 2 * count], refs[2 * count : 3 * count]
    in_sem, out_sem = refs[3 * count :]
    loads = [pltpu.make_async_copy(ins[i], bufs[i], in_sem.at[i]) for i in range(count)]
    stores = [pltpu.make_async_copy(bufs[i], outs[i], out_sem.at[i]) for i in range(count)]
    for load in loads:
        load.start()
    for load, store in zip(loads, stores):
        load.wait()
        store.start()
    for store in stores:
        store.wait()


def body(geo, tokens, cotangent, picks, gates, w_gate, w_up, w_down):
    nx, nzh, nzl, ny, nc = geo
    ne, slots = picks.shape[1], picks.shape[2]
    nb = nx * nzh
    n = nb * ne
    tdev, model = tokens.shape
    wide, ff = w_gate.shape[1], w_gate.shape[2]
    half, hw = ne * 4, 3 * ff // 2
    vm = pl.BlockSpec(memory_space=pltpu.VMEM)
    hbm = pl.BlockSpec(memory_space=pl.ANY)
    results = (
        jax.ShapeDtypeStruct((tdev, model), BF16),
        jax.ShapeDtypeStruct((tdev, model), BF16),
        jax.ShapeDtypeStruct((slots, ne), F32),
        jax.ShapeDtypeStruct((wide, ff), BF16),
        jax.ShapeDtypeStruct((wide, ff), BF16),
        jax.ShapeDtypeStruct((ff, wide), BF16),
    )
    outs = pl.pallas_call(
        functools.partial(kernel, geo),
        out_shape=results,
        in_specs=[hbm, hbm, vm, vm, hbm, hbm, hbm],
        out_specs=(hbm, hbm, vm, hbm, hbm, hbm),
        scratch_shapes=[
            pltpu.VMEM((tdev, model), BF16),
            pltpu.VMEM((tdev, model), BF16),
            pltpu.VMEM((wide, ff), BF16),
            pltpu.VMEM((wide, ff), BF16),
            pltpu.VMEM((ff, wide), BF16),
            pltpu.VMEM((tdev, model), BF16),
            pltpu.VMEM((tdev, model), BF16),
            pltpu.VMEM((wide, ff), BF16),
            pltpu.VMEM((wide, ff), BF16),
            pltpu.VMEM((ff, wide), BF16),
            pltpu.VMEM((n, 8, wide), BF16),
            pltpu.VMEM((n, 8, wide), BF16),
            pltpu.VMEM((nb, half, wide), BF16),
            pltpu.VMEM((nb, half, wide), BF16),
            pltpu.VMEM((nb, 2, half, hw), BF16),
            pltpu.VMEM((2, 2, 2, half, hw), BF16),
            pltpu.VMEM((2, 2, half, hw), BF16),
            pltpu.VMEM((2, 2, half, hw), BF16),
            pltpu.VMEM((2, 2, half, hw), BF16),
            pltpu.VMEM((2, 2, half, hw), BF16),
            pltpu.VMEM((nb, 2, half, hw), BF16),
            pltpu.VMEM((n, 8, wide), BF16),
            pltpu.SemaphoreType.DMA((5,)),
            pltpu.SemaphoreType.DMA((5,)),
            pltpu.SemaphoreType.DMA,
            pltpu.SemaphoreType.DMA((nb,)),
            pltpu.SemaphoreType.DMA((2, 2, 3)),
            pltpu.SemaphoreType.DMA((2, 2, 3)),
            pltpu.SemaphoreType.DMA((2, 2)),
            pltpu.SemaphoreType.DMA((2, 2)),
            pltpu.SemaphoreType.DMA((2, 2, 3)),
            pltpu.SemaphoreType.DMA((2, 2, 3)),
            pltpu.SemaphoreType.DMA,
            pltpu.SemaphoreType.DMA((nb,)),
        ],
        compiler_params=pltpu.CompilerParams(
            collective_id=0, has_side_effects=True, vmem_limit_bytes=62 * 1024 * 1024
        ),
        name="moe",
    )(
        tokens, cotangent, picks[0].T, gates[0].T,
        w_gate[0], w_up[0], w_down[0],
    )
    outs = pl.pallas_call(
        hand_on,
        out_shape=results,
        in_specs=[hbm] * 6,
        out_specs=(hbm,) * 6,
        scratch_shapes=[pltpu.VMEM(r.shape, r.dtype) for r in results]
        + [pltpu.SemaphoreType.DMA((6,)), pltpu.SemaphoreType.DMA((6,))],
        compiler_params=pltpu.CompilerParams(vmem_limit_bytes=62 * 1024 * 1024),
        name="hand_on",
    )(*outs)
    mixed, tgrad, ggrad, gwg, gwu, gwd = outs
    return (mixed, tgrad, ggrad.T[None], gwg[None], gwu[None], gwd[None])


def solution(mesh):
    ne = mesh.shape["expert"]
    geo = (4, 2, 4, 4, 2) if ne == 32 else (4, 2, 1, 1, ne)
    return jax.shard_map(
        functools.partial(body, geo),
        mesh=mesh,
        in_specs=(
            P(("dp", "expert"), None),
            P(("dp", "expert"), None),
            P(("dp", "expert"), None, None),
            P(("dp", "expert"), None, None),
            P("expert", "dp", None),
            P("expert", "dp", None),
            P("expert", None, "dp"),
        ),
        out_specs=(
            P(("dp", "expert"), None),
            P(("dp", "expert"), None),
            P(("dp", "expert"), None, None),
            P("expert", "dp", None),
            P("expert", "dp", None),
            P("expert", None, "dp"),
        ),
        check_vma=False,
    )
```

```python
import functools

import jax
import jax.numpy as jnp
from jax import lax
from jax.experimental import pallas as pl
from jax.experimental.pallas import tpu as pltpu
from jax.sharding import PartitionSpec as P

MESH = pl.DeviceIdType.MESH
F32 = jnp.float32
BF16 = jnp.bfloat16
GREET = 5


def nn(a, b):
    return lax.dot_general(a, b, (((1,), (0,)), ((), ())), preferred_element_type=F32)


def nt(a, b):
    return lax.dot_general(a, b, (((1,), (1,)), ((), ())), preferred_element_type=F32)


def tn(a, b):
    return lax.dot_general(a, b, (((0,), (0,)), ((), ())), preferred_element_type=F32)


def select_rows(rows, cols, shift):
    i = lax.broadcasted_iota(jnp.int32, (rows, cols), 0)
    c = lax.broadcasted_iota(jnp.int32, (rows, cols), 1)
    want = (i // 4) * 8 + i % 4 + shift
    return (want == c).astype(BF16)


def place_rows(rows, cols, shift):
    i = lax.broadcasted_iota(jnp.int32, (rows, cols), 1)
    c = lax.broadcasted_iota(jnp.int32, (rows, cols), 0)
    want = (i // 4) * 8 + i % 4 + shift
    return (want == c).astype(BF16)


def kernel(
    geo,
    tok_in, cot_in, pick_in, gate_in, wg_in, wu_in, wd_in,
    mixed_out, tgrad_out, ggrad, gwg_out, gwu_out, gwd_out,
    tok, cot, wg, wu, wd, mixed, tgrad, gwg, gwu, gwd,
    sbuf, rbuf, xs, ys, terms, s1, t1, s2, s3, zb_out, ag, bbuf,
    in_sem, out_sem, a2a_send, a2a_recv, rs_send, rs_recv, z_send, z_recv, ag_send, ag_recv,
    cb_send, cb_recv,
):
    nx, nzh, nzl, ny, nc = geo
    ne = nzl * ny * nc
    nb = nx * nzh
    n = nb * ne
    nz = nzh * nzl
    per = nz * ny * nc
    rows = ne * 8
    half = ne * 4
    tdev = tok.shape[0]
    wide = wg.shape[0]
    ff = wg.shape[1]
    hw = 3 * ff // 2
    hf = ff // 2
    dp = lax.axis_index("dp")
    ex = lax.axis_index("expert")
    me = dp * ne + ex
    x, zh = lax.div(dp, nzh), lax.rem(dp, nzh)
    core = lax.rem(ex, nc)
    yy = lax.rem(lax.div(ex, nc), ny)
    zl = lax.div(ex, nc * ny)
    zz = zh * nzl + zl

    loads = [
        pltpu.make_async_copy(src, dst, in_sem.at[i])
        for i, (src, dst) in enumerate(
            ((tok_in, tok), (cot_in, cot), (wg_in, wg), (wu_in, wu), (wd_in, wd))
        )
    ]
    barrier = pltpu.get_barrier_semaphore()
    for load in loads:
        load.start()

    def greet(i, carry):
        other = lax.rem(me + i, n)
        pl.semaphore_signal(barrier, inc=1, device_id=other, device_id_type=pl.DeviceIdType.LOGICAL)
        return carry

    lax.fori_loop(1, n, greet, 0, unroll=GREET)

    pick_x = select_rows(half, rows, 0)
    pick_y = select_rows(half, rows, 4)
    put_x = place_rows(rows, half, 0)
    put_y = place_rows(rows, half, 4)
    eye = lax.broadcasted_iota(jnp.int32, (half, half), 0) == lax.broadcasted_iota(
        jnp.int32, (half, half), 1
    )
    slot = lax.broadcasted_iota(jnp.int32, (4, half), 0) == lax.rem(
        lax.broadcasted_iota(jnp.int32, (4, half), 1), 4
    )
    spread = (
        lax.broadcasted_iota(jnp.int32, (ne, half), 0)
        == lax.div(lax.broadcasted_iota(jnp.int32, (ne, half), 1), 4)
    ).astype(BF16)

    def pieces(v):
        top = v.astype(BF16)
        rest = v - top.astype(F32)
        mid = rest.astype(BF16)
        return top, mid, (rest - mid.astype(F32)).astype(BF16)

    def in_row(v):
        top, mid, low = pieces(v)
        wide_v = nn(top, spread) + nn(mid, spread) + nn(low, spread)
        return jnp.sum(jnp.where(slot, wide_v, 0.0), axis=0, keepdims=True)

    pick_row = in_row(pick_in[...].astype(F32)).astype(jnp.int32)
    gate_row = in_row(gate_in[...])
    pick_col = jnp.sum(jnp.where(eye, pick_row, 0), axis=1, keepdims=True)
    gate_col = jnp.sum(jnp.where(eye, gate_row, 0.0), axis=1, keepdims=True)
    hot = (lax.broadcasted_iota(jnp.int32, (half, tdev), 1) == pick_col).astype(BF16)

    def gather(k, carry):
        at = pl.ds(pl.multiple_of(k * wide, 128), wide)
        token_rows = nn(hot, tok[:, at]).astype(BF16)
        grad_rows = (nn(hot, cot[:, at]) * gate_col).astype(BF16)
        both = nn(put_x, token_rows) + nn(put_y, grad_rows)
        sbuf[pl.ds(k * ne, ne)] = both.reshape(ne, 8, wide).astype(BF16)
        return carry

    loads[0].wait()
    loads[1].wait()
    lax.fori_loop(0, nb, gather, 0)
    pl.semaphore_wait(barrier, n - 1)

    def dispatch(ways, first):
        def send(i, carry):
            dx = ways[0]
            if len(ways) == 2:
                dx = ways[0] + (ways[1] - ways[0]) * lax.rem(i, 2)
            o = lax.rem(lax.div(i, len(ways)) * 37, per)
            dc, r = lax.rem(o, nc), lax.div(o, nc)
            dz, dy = lax.rem(r, nz), lax.div(r, nz)
            pz = lax.rem(zz + dz, nz)
            pdp = lax.rem(x + dx, nx) * nzh + lax.div(pz, nzl)
            pex = (lax.rem(pz, nzl) * ny + lax.rem(yy + dy, ny)) * nc + lax.rem(core + dc, nc)
            pltpu.make_async_remote_copy(
                src_ref=sbuf.at[pdp * ne + pex], dst_ref=rbuf.at[me],
                send_sem=a2a_send, recv_sem=a2a_recv.at[dp],
                device_id=(pdp, pex), device_id_type=MESH,
            ).start()
            return carry

        lax.fori_loop(first, per * len(ways), send, 0)

    dispatch((2,), 0)
    dispatch((1, 3), 0)
    dispatch((0,), 1)
    pltpu.make_async_copy(sbuf.at[me], rbuf.at[me], a2a_recv.at[dp]).start()

    def sent(src, send_sem):
        part = src.at[pl.ds(0, n - 1)]
        pltpu.make_async_copy(part, part, send_sem).wait()

    def products(b):
        part = rbuf.at[pl.ds(b * ne, ne)]
        pltpu.make_async_copy(part, part, a2a_recv.at[b]).wait()
        z = rbuf[pl.ds(b * ne, ne)].reshape(rows, wide)
        xb = nn(pick_x, z).astype(BF16)
        yb = nn(pick_y, z).astype(BF16)
        xs[b] = xb
        ys[b] = yb
        terms[b, 0, :, :ff] = nn(xb, wg[...]).astype(BF16)
        up = nn(xb, wu[...]).astype(BF16)
        terms[b, 0, :, ff:] = up[:, :hf]
        terms[b, 1, :, :hf] = up[:, hf:]
        terms[b, 1, :, hf:] = nt(yb, wd[...]).astype(BF16)

    to = (lax.rem(x + 1, nx), lax.rem(x + nx - 1, nx))
    come = (to[1], to[0])
    opposite = lax.rem(x + 2, nx)
    side = (zh, 1 - zh)

    def blk(q, s):
        return q * nzh + s

    def remote(src, dst, send_sem, recv_sem, pdp):
        copy = pltpu.make_async_remote_copy(
            src_ref=src, dst_ref=dst, send_sem=send_sem, recv_sem=recv_sem,
            device_id=(pdp, ex), device_id_type=MESH,
        )
        copy.start()
        return copy

    def wait_for(dst, sem):
        pltpu.make_async_copy(dst, dst, sem).wait()

    sends = []

    def rs_first(c):
        for h in (0, 1):
            sends.append(remote(terms.at[blk(opposite, side[c]), h], s1.at[c, h, 1],
                                rs_send.at[c, h, 0], rs_recv.at[c, h, 0], blk(to[h], zh)))

    def rs_pass(c):
        for h in (0, 1):
            sends.append(remote(terms.at[blk(to[h], side[c]), 1 - h], s1.at[c, 1 - h, 0],
                                rs_send.at[c, h, 1], rs_recv.at[c, 1 - h, 1], blk(to[h], zh)))
        for h in (0, 1):
            wait_for(s1.at[c, h, 1], rs_recv.at[c, h, 0])
            t1[c, h] = (terms[blk(to[h], side[c]), h].astype(F32) + s1[c, h, 1].astype(F32)).astype(BF16)
            sends.append(remote(t1.at[c, h], s2.at[c, h], rs_send.at[c, h, 2], rs_recv.at[c, h, 2],
                                blk(to[h], zh)))

    def rs_total(c, h):
        wait_for(s1.at[c, h, 0], rs_recv.at[c, h, 1])
        wait_for(s2.at[c, h], rs_recv.at[c, h, 2])
        return (terms[blk(x, side[c]), h].astype(F32) + s1[c, h, 0].astype(F32)
                + s2[c, h].astype(F32))

    def products_of(first, gap, count):
        def one(i, carry):
            products(blk(lax.rem(first + gap * lax.div(i, nzh), nx), lax.rem(i, nzh)))
            return carry

        lax.fori_loop(0, count * nzh, one, 0)

    zpeer = blk(x, 1 - zh)

    def z_exchange(c, h):
        sends.append(remote(zb_out.at[c, h], s3.at[c, h], z_send.at[c, h], z_recv.at[c, h], zpeer))

    for load in loads[2:]:
        load.wait()
    products_of(opposite, 0, 1)
    rs_first(0)
    rs_first(1)
    products_of(x + 1, 2, 2)
    rs_pass(0)
    rs_pass(1)
    products_of(x, 0, 1)
    for c in (0, 1):
        for h in (0, 1):
            zb_out[c, h] = rs_total(c, h).astype(BF16)
            if c == 0:
                z_exchange(c, h)
    for h in (0, 1):
        wait_for(s3.at[0, h], z_recv.at[0, h])
        z_exchange(1, h)
    sent(sbuf, a2a_send)

    step = half // 4

    def activate(b, c):
        def part(i, carry):
            at = pl.ds(pl.multiple_of(i * step, step), step)
            lo = zb_out[1 - c, 0, at, :].astype(F32) + s3[c, 0, at, :].astype(F32)
            hi = zb_out[1 - c, 1, at, :].astype(F32) + s3[c, 1, at, :].astype(F32)
            gate = lo[:, :ff]
            up = jnp.concatenate([lo[:, ff:], hi[:, :hf]], axis=1)
            back = hi[:, hf:]
            sig = 1.0 / (1.0 + jnp.exp(-gate))
            silu = gate * sig
            hidden = (silu * up).astype(BF16)
            g_up = (back * silu).astype(BF16)
            g_gate = (back * up * sig * (1.0 + gate * (1.0 - sig))).astype(BF16)
            ag[b, 0, at, :ff] = hidden
            ag[b, 0, at, ff:] = g_gate[:, :hf]
            ag[b, 1, at, :hf] = g_gate[:, hf:]
            ag[b, 1, at, hf:] = g_up
            return carry

        lax.fori_loop(0, 4, part, 0)

    def ag_first(c, s, g):
        mine = blk(x, s)
        for h in (g, 1 - g):
            j = 0 if g == h else 1
            sends.append(remote(ag.at[mine, g], ag.at[mine, g], ag_send.at[c, h, j],
                                ag_recv.at[c, h, j], blk(to[h], zh)))

    def ag_pass(c, s):
        for h in (0, 1):
            got = blk(come[h], s)
            wait_for(ag.at[got, h], ag_recv.at[c, h, 0])
            sends.append(remote(ag.at[got, h], ag.at[got, h], ag_send.at[c, h, 2],
                                ag_recv.at[c, h, 2], blk(to[h], zh)))

    def outputs(b):
        out = nn(ag[b, 0, :, :ff], wd[...]).astype(BF16)
        grad = nt(ag[b, 0, :, ff:], wg[:, :hf]) + nt(ag[b, 1, :, :hf], wg[:, hf:])
        grad = (grad + nt(ag[b, 1, :, hf:], wu[...])).astype(BF16)
        both = nn(put_x, out) + nn(put_y, grad)
        sbuf[pl.ds(b * ne, ne)] = both.reshape(ne, 8, wide).astype(BF16)

    def ship(b, first):
        def send(i, carry):
            o = lax.rem(i * 13, ne)
            dc, r = lax.rem(o, nc), lax.div(o, nc)
            dy, dz = lax.rem(r, ny), lax.div(r, ny)
            pex = (lax.rem(zl + dz, nzl) * ny + lax.rem(yy + dy, ny)) * nc + lax.rem(core + dc, nc)
            pltpu.make_async_remote_copy(
                src_ref=sbuf.at[b * ne + pex], dst_ref=bbuf.at[me],
                send_sem=cb_send, recv_sem=cb_recv.at[dp],
                device_id=(b, pex), device_id_type=MESH,
            ).start()
            return carry

        lax.fori_loop(first, ne, send, 0)

    def beside(s, *steps):
        def one(i, carry):
            for step in steps:
                step(blk(lax.rem(x + 1 + 2 * i, nx), s))
            return carry

        lax.fori_loop(0, 2, one, 0)

    def ship_all(b):
        ship(b, 0)

    def ag_side(c, s):
        for h in (0, 1):
            wait_for(ag.at[blk(come[h], s), 1 - h], ag_recv.at[c, h, 1])

    def ag_far(c, s):
        for h in (0, 1):
            wait_for(ag.at[blk(opposite, s), h], ag_recv.at[c, h, 2])

    activate(zpeer, 0)
    ag_first(0, 1 - zh, 0)
    ag_first(0, 1 - zh, 1)
    outputs(zpeer)
    ag_pass(0, 1 - zh)
    ag_side(0, 1 - zh)
    beside(1 - zh, outputs)
    ag_far(0, 1 - zh)
    outputs(blk(opposite, 1 - zh))
    for h in (0, 1):
        wait_for(s3.at[1, h], z_recv.at[1, h])
    ship_all(zpeer)
    activate(dp, 1)
    ag_first(1, zh, 0)
    ag_first(1, zh, 1)
    beside(1 - zh, ship_all)
    ship_all(blk(opposite, 1 - zh))
    outputs(dp)
    ship(dp, 1)
    pltpu.make_async_copy(sbuf.at[me], bbuf.at[me], cb_recv.at[dp]).start()
    ag_pass(1, zh)
    ag_side(1, zh)
    beside(zh, outputs, ship_all)
    ag_far(1, zh)
    outputs(blk(opposite, zh))
    ship_all(blk(opposite, zh))

    all_rows = nb * half

    def grads_in(m, carry):
        at = pl.ds(pl.multiple_of(m * 128, 128), 128)
        xt = xs[:, :, at].reshape(all_rows, 128)
        gwg[at, :hf] = tn(xt, ag[:, 0, :, ff:].reshape(all_rows, hf)).astype(BF16)
        rest = tn(xt, ag[:, 1, :, :].reshape(all_rows, hw))
        gwg[at, hf:] = rest[:, :hf].astype(BF16)
        gwu[at, :] = rest[:, hf:].astype(BF16)
        return carry

    lax.fori_loop(0, wide // 128, grads_in, 0)

    def grads_down(m, carry):
        at = pl.ds(pl.multiple_of(m * 128, 128), 128)
        ht = ag[:, 0, :, at].reshape(all_rows, 128)
        gwd[at, :] = tn(ht, ys[...].reshape(all_rows, wide)).astype(BF16)
        return carry

    lax.fori_loop(0, ff // 128, grads_down, 0)

    stores = [
        pltpu.make_async_copy(src, dst, out_sem.at[i])
        for i, (src, dst) in enumerate(((gwg, gwg_out), (gwu, gwu_out), (gwd, gwd_out)))
    ]
    for store in stores:
        store.start()

    here = lax.broadcasted_iota(jnp.int32, (tdev, half), 0) == pick_row
    to_grad = nn(here.astype(BF16), pick_y).astype(BF16)
    weight = jnp.where(here, gate_row, 0.0)
    w_hi = weight.astype(BF16)
    w_lo = nn((weight - w_hi.astype(F32)).astype(BF16), pick_x).astype(BF16)
    w_hi = nn(w_hi, pick_x).astype(BF16)

    def combine(i, prods):
        j = lax.rem(i, nx)
        j = j + lax.div(j, 2) * (1 - 2 * lax.rem(j, 2))
        s = lax.rem(zh + lax.div(i, nx), nzh)
        k = blk(lax.rem(x + j, nx), s)
        part = bbuf.at[pl.ds(k * ne, ne)]
        pltpu.make_async_copy(part, part, cb_recv.at[k]).wait()
        at = pl.ds(pl.multiple_of(k * wide, 128), wide)
        z = bbuf[pl.ds(k * ne, ne)].reshape(rows, wide)
        mixed[:, at] = (nn(w_hi, z) + nn(w_lo, z)).astype(BF16)
        tgrad[:, at] = nn(to_grad, z).astype(BF16)
        pltpu.make_async_copy(mixed.at[:, at], mixed_out.at[:, at], out_sem.at[3]).start()
        pltpu.make_async_copy(tgrad.at[:, at], tgrad_out.at[:, at], out_sem.at[4]).start()
        return prods + nt(cot[:, at], nn(pick_x, z).astype(BF16))

    prods = lax.fori_loop(0, nb, combine, jnp.zeros((tdev, half), F32))
    total = jnp.sum(jnp.where(here, prods, 0.0), axis=0, keepdims=True)
    top, mid, low = pieces(jnp.where(slot, total, 0.0))
    ggrad[...] = nt(top, spread) + nt(mid, spread) + nt(low, spread)
    for store in stores:
        store.wait()
    pltpu.make_async_copy(mixed, mixed_out, out_sem.at[3]).wait()
    pltpu.make_async_copy(tgrad, tgrad_out, out_sem.at[4]).wait()
    for copy in sends:
        copy.wait_send()
    sent(sbuf, cb_send)


def hand_on(*refs):
    count = (len(refs) - 2) // 3
    ins, outs, bufs = refs[:count], refs[count : 2 * count], refs[2 * count : 3 * count]
    in_sem, out_sem = refs[3 * count :]
    loads = [pltpu.make_async_copy(ins[i], bufs[i], in_sem.at[i]) for i in range(count)]
    stores = [pltpu.make_async_copy(bufs[i], outs[i], out_sem.at[i]) for i in range(count)]
    for load in loads:
        load.start()
    for load, store in zip(loads, stores):
        load.wait()
        store.start()
    for store in stores:
        store.wait()


def body(geo, tokens, cotangent, picks, gates, w_gate, w_up, w_down):
    nx, nzh, nzl, ny, nc = geo
    ne, slots = picks.shape[1], picks.shape[2]
    nb = nx * nzh
    n = nb * ne
    tdev, model = tokens.shape
    wide, ff = w_gate.shape[1], w_gate.shape[2]
    half, hw = ne * 4, 3 * ff // 2
    vm = pl.BlockSpec(memory_space=pltpu.VMEM)
    hbm = pl.BlockSpec(memory_space=pl.ANY)
    results = (
        jax.ShapeDtypeStruct((tdev, model), BF16),
        jax.ShapeDtypeStruct((tdev, model), BF16),
        jax.ShapeDtypeStruct((slots, ne), F32),
        jax.ShapeDtypeStruct((wide, ff), BF16),
        jax.ShapeDtypeStruct((wide, ff), BF16),
        jax.ShapeDtypeStruct((ff, wide), BF16),
    )
    outs = pl.pallas_call(
        functools.partial(kernel, geo),
        out_shape=results,
        in_specs=[hbm, hbm, vm, vm, hbm, hbm, hbm],
        out_specs=(hbm, hbm, vm, hbm, hbm, hbm),
        scratch_shapes=[
            pltpu.VMEM((tdev, model), BF16),
            pltpu.VMEM((tdev, model), BF16),
            pltpu.VMEM((wide, ff), BF16),
            pltpu.VMEM((wide, ff), BF16),
            pltpu.VMEM((ff, wide), BF16),
            pltpu.VMEM((tdev, model), BF16),
            pltpu.VMEM((tdev, model), BF16),
            pltpu.VMEM((wide, ff), BF16),
            pltpu.VMEM((wide, ff), BF16),
            pltpu.VMEM((ff, wide), BF16),
            pltpu.VMEM((n, 8, wide), BF16),
            pltpu.VMEM((n, 8, wide), BF16),
            pltpu.VMEM((nb, half, wide), BF16),
            pltpu.VMEM((nb, half, wide), BF16),
            pltpu.VMEM((nb, 2, half, hw), BF16),
            pltpu.VMEM((2, 2, 2, half, hw), BF16),
            pltpu.VMEM((2, 2, half, hw), BF16),
            pltpu.VMEM((2, 2, half, hw), BF16),
            pltpu.VMEM((2, 2, half, hw), BF16),
            pltpu.VMEM((2, 2, half, hw), BF16),
            pltpu.VMEM((nb, 2, half, hw), BF16),
            pltpu.VMEM((n, 8, wide), BF16),
            pltpu.SemaphoreType.DMA((5,)),
            pltpu.SemaphoreType.DMA((5,)),
            pltpu.SemaphoreType.DMA,
            pltpu.SemaphoreType.DMA((nb,)),
            pltpu.SemaphoreType.DMA((2, 2, 3)),
            pltpu.SemaphoreType.DMA((2, 2, 3)),
            pltpu.SemaphoreType.DMA((2, 2)),
            pltpu.SemaphoreType.DMA((2, 2)),
            pltpu.SemaphoreType.DMA((2, 2, 3)),
            pltpu.SemaphoreType.DMA((2, 2, 3)),
            pltpu.SemaphoreType.DMA,
            pltpu.SemaphoreType.DMA((nb,)),
        ],
        compiler_params=pltpu.CompilerParams(
            collective_id=0, has_side_effects=True, vmem_limit_bytes=62 * 1024 * 1024
        ),
        name="moe",
    )(
        tokens, cotangent, picks[0].T, gates[0].T,
        w_gate[0], w_up[0], w_down[0],
    )
    outs = pl.pallas_call(
        hand_on,
        out_shape=results,
        in_specs=[hbm] * 6,
        out_specs=(hbm,) * 6,
        scratch_shapes=[pltpu.VMEM(r.shape, r.dtype) for r in results]
        + [pltpu.SemaphoreType.DMA((6,)), pltpu.SemaphoreType.DMA((6,))],
        compiler_params=pltpu.CompilerParams(vmem_limit_bytes=62 * 1024 * 1024),
        name="hand_on",
    )(*outs)
    mixed, tgrad, ggrad, gwg, gwu, gwd = outs
    return (mixed, tgrad, ggrad.T[None], gwg[None], gwu[None], gwd[None])


def solution(mesh):
    ne = mesh.shape["expert"]
    geo = (4, 2, 4, 4, 2) if ne == 32 else (4, 2, 1, 1, ne)
    return jax.shard_map(
        functools.partial(body, geo),
        mesh=mesh,
        in_specs=(
            P(("dp", "expert"), None),
            P(("dp", "expert"), None),
            P(("dp", "expert"), None, None),
            P(("dp", "expert"), None, None),
            P("expert", "dp", None),
            P("expert", "dp", None),
            P("expert", None, "dp"),
        ),
        out_specs=(
            P(("dp", "expert"), None),
            P(("dp", "expert"), None),
            P(("dp", "expert"), None, None),
            P("expert", "dp", None),
            P("expert", "dp", None),
            P("expert", None, "dp"),
        ),
        check_vma=False,
    )
```

```python
import functools

import jax
import jax.numpy as jnp
from jax import lax
from jax.experimental import pallas as pl
from jax.experimental.pallas import tpu as pltpu
from jax.sharding import PartitionSpec as P

MESH = pl.DeviceIdType.MESH
F32 = jnp.float32
BF16 = jnp.bfloat16
GREET = 5


def nn(a, b):
    return lax.dot_general(a, b, (((1,), (0,)), ((), ())), preferred_element_type=F32)


def nt(a, b):
    return lax.dot_general(a, b, (((1,), (1,)), ((), ())), preferred_element_type=F32)


def tn(a, b):
    return lax.dot_general(a, b, (((0,), (0,)), ((), ())), preferred_element_type=F32)


def select_rows(rows, cols, shift):
    i = lax.broadcasted_iota(jnp.int32, (rows, cols), 0)
    c = lax.broadcasted_iota(jnp.int32, (rows, cols), 1)
    want = (i // 4) * 8 + i % 4 + shift
    return (want == c).astype(BF16)


def place_rows(rows, cols, shift):
    i = lax.broadcasted_iota(jnp.int32, (rows, cols), 1)
    c = lax.broadcasted_iota(jnp.int32, (rows, cols), 0)
    want = (i // 4) * 8 + i % 4 + shift
    return (want == c).astype(BF16)


def kernel(
    geo,
    tok_in, cot_in, pick_in, gate_in, wg_in, wu_in, wd_in,
    mixed_out, tgrad_out, ggrad, gwg_out, gwu_out, gwd_out,
    tok, cot, wg, wu, wd, mixed, tgrad, gwg, gwu, gwd,
    sbuf, rbuf, xs, ys, terms, s1, t1, s2, s3, zb_out, ag, bbuf,
    in_sem, out_sem, a2a_send, a2a_recv, rs_send, rs_recv, z_send, z_recv, ag_send, ag_recv,
    cb_send, cb_recv,
):
    nx, nzh, nzl, ny, nc = geo
    ne = nzl * ny * nc
    nb = nx * nzh
    n = nb * ne
    nz = nzh * nzl
    per = nz * ny * nc
    rows = ne * 8
    half = ne * 4
    tdev = tok.shape[0]
    wide = wg.shape[0]
    ff = wg.shape[1]
    hw = 3 * ff // 2
    hf = ff // 2
    dp = lax.axis_index("dp")
    ex = lax.axis_index("expert")
    me = dp * ne + ex
    x, zh = lax.div(dp, nzh), lax.rem(dp, nzh)
    core = lax.rem(ex, nc)
    yy = lax.rem(lax.div(ex, nc), ny)
    zl = lax.div(ex, nc * ny)
    zz = zh * nzl + zl

    loads = [
        pltpu.make_async_copy(src, dst, in_sem.at[i])
        for i, (src, dst) in enumerate(
            ((tok_in, tok), (cot_in, cot), (wg_in, wg), (wu_in, wu), (wd_in, wd))
        )
    ]
    barrier = pltpu.get_barrier_semaphore()
    for load in loads:
        load.start()

    def greet(i, carry):
        other = lax.rem(me + i, n)
        pl.semaphore_signal(barrier, inc=1, device_id=other, device_id_type=pl.DeviceIdType.LOGICAL)
        return carry

    lax.fori_loop(1, n, greet, 0, unroll=GREET)

    pick_x = select_rows(half, rows, 0)
    pick_y = select_rows(half, rows, 4)
    put_x = place_rows(rows, half, 0)
    put_y = place_rows(rows, half, 4)
    eye = lax.broadcasted_iota(jnp.int32, (half, half), 0) == lax.broadcasted_iota(
        jnp.int32, (half, half), 1
    )
    slot = lax.broadcasted_iota(jnp.int32, (4, half), 0) == lax.rem(
        lax.broadcasted_iota(jnp.int32, (4, half), 1), 4
    )
    spread = (
        lax.broadcasted_iota(jnp.int32, (ne, half), 0)
        == lax.div(lax.broadcasted_iota(jnp.int32, (ne, half), 1), 4)
    ).astype(BF16)

    def pieces(v):
        top = v.astype(BF16)
        rest = v - top.astype(F32)
        mid = rest.astype(BF16)
        return top, mid, (rest - mid.astype(F32)).astype(BF16)

    def in_row(v):
        top, mid, low = pieces(v)
        wide_v = nn(top, spread) + nn(mid, spread) + nn(low, spread)
        return jnp.sum(jnp.where(slot, wide_v, 0.0), axis=0, keepdims=True)

    pick_row = in_row(pick_in[...].astype(F32)).astype(jnp.int32)
    gate_row = in_row(gate_in[...])
    pick_col = jnp.sum(jnp.where(eye, pick_row, 0), axis=1, keepdims=True)
    gate_col = jnp.sum(jnp.where(eye, gate_row, 0.0), axis=1, keepdims=True)
    hot = (lax.broadcasted_iota(jnp.int32, (half, tdev), 1) == pick_col).astype(BF16)

    def gather(k, carry):
        at = pl.ds(pl.multiple_of(k * wide, 128), wide)
        token_rows = nn(hot, tok[:, at]).astype(BF16)
        grad_rows = (nn(hot, cot[:, at]) * gate_col).astype(BF16)
        both = nn(put_x, token_rows) + nn(put_y, grad_rows)
        sbuf[pl.ds(k * ne, ne)] = both.reshape(ne, 8, wide).astype(BF16)
        return carry

    loads[0].wait()
    loads[1].wait()
    lax.fori_loop(0, nb, gather, 0)
    pl.semaphore_wait(barrier, n - 1)

    def dispatch(ways, first):
        def send(i, carry):
            dx = ways[0]
            if len(ways) == 2:
                dx = ways[0] + (ways[1] - ways[0]) * lax.rem(i, 2)
            o = lax.rem(lax.div(i, len(ways)) * 37, per)
            dc, r = lax.rem(o, nc), lax.div(o, nc)
            dz, dy = lax.rem(r, nz), lax.div(r, nz)
            pz = lax.rem(zz + dz, nz)
            pdp = lax.rem(x + dx, nx) * nzh + lax.div(pz, nzl)
            pex = (lax.rem(pz, nzl) * ny + lax.rem(yy + dy, ny)) * nc + lax.rem(core + dc, nc)
            pltpu.make_async_remote_copy(
                src_ref=sbuf.at[pdp * ne + pex], dst_ref=rbuf.at[me],
                send_sem=a2a_send, recv_sem=a2a_recv.at[dp],
                device_id=(pdp, pex), device_id_type=MESH,
            ).start()
            return carry

        lax.fori_loop(first, per * len(ways), send, 0)

    dispatch((2,), 0)
    dispatch((1, 3), 0)
    pltpu.make_async_copy(sbuf.at[me], rbuf.at[me], a2a_recv.at[dp]).start()

    def sent(src, send_sem):
        part = src.at[pl.ds(0, n - 1)]
        pltpu.make_async_copy(part, part, send_sem).wait()

    def products(b):
        part = rbuf.at[pl.ds(b * ne, ne)]
        pltpu.make_async_copy(part, part, a2a_recv.at[b]).wait()
        z = rbuf[pl.ds(b * ne, ne)].reshape(rows, wide)
        xb = nn(pick_x, z).astype(BF16)
        yb = nn(pick_y, z).astype(BF16)
        xs[b] = xb
        ys[b] = yb
        terms[b, 0, :, :ff] = nn(xb, wg[...]).astype(BF16)
        up = nn(xb, wu[...]).astype(BF16)
        terms[b, 0, :, ff:] = up[:, :hf]
        terms[b, 1, :, :hf] = up[:, hf:]
        terms[b, 1, :, hf:] = nt(yb, wd[...]).astype(BF16)

    to = (lax.rem(x + 1, nx), lax.rem(x + nx - 1, nx))
    come = (to[1], to[0])
    opposite = lax.rem(x + 2, nx)
    side = (zh, 1 - zh)

    def blk(q, s):
        return q * nzh + s

    def remote(src, dst, send_sem, recv_sem, pdp):
        copy = pltpu.make_async_remote_copy(
            src_ref=src, dst_ref=dst, send_sem=send_sem, recv_sem=recv_sem,
            device_id=(pdp, ex), device_id_type=MESH,
        )
        copy.start()
        return copy

    def wait_for(dst, sem):
        pltpu.make_async_copy(dst, dst, sem).wait()

    sends = []

    def rs_first(c):
        for h in (0, 1):
            sends.append(remote(terms.at[blk(opposite, side[c]), h], s1.at[c, h, 1],
                                rs_send.at[c, h, 0], rs_recv.at[c, h, 0], blk(to[h], zh)))

    def rs_pass(c):
        for h in (0, 1):
            sends.append(remote(terms.at[blk(to[h], side[c]), 1 - h], s1.at[c, 1 - h, 0],
                                rs_send.at[c, h, 1], rs_recv.at[c, 1 - h, 1], blk(to[h], zh)))
        for h in (0, 1):
            wait_for(s1.at[c, h, 1], rs_recv.at[c, h, 0])
            t1[c, h] = (terms[blk(to[h], side[c]), h].astype(F32) + s1[c, h, 1].astype(F32)).astype(BF16)
            sends.append(remote(t1.at[c, h], s2.at[c, h], rs_send.at[c, h, 2], rs_recv.at[c, h, 2],
                                blk(to[h], zh)))

    def rs_total(c, h):
        wait_for(s1.at[c, h, 0], rs_recv.at[c, h, 1])
        wait_for(s2.at[c, h], rs_recv.at[c, h, 2])
        return (terms[blk(x, side[c]), h].astype(F32) + s1[c, h, 0].astype(F32)
                + s2[c, h].astype(F32))

    def products_of(first, gap, count):
        def one(i, carry):
            products(blk(lax.rem(first + gap * lax.div(i, nzh), nx), lax.rem(i, nzh)))
            return carry

        lax.fori_loop(0, count * nzh, one, 0)

    zpeer = blk(x, 1 - zh)

    def z_exchange(c, h):
        sends.append(remote(zb_out.at[c, h], s3.at[c, h], z_send.at[c, h], z_recv.at[c, h], zpeer))

    for load in loads[2:]:
        load.wait()
    products_of(opposite, 0, 1)
    rs_first(0)
    rs_first(1)
    dispatch((0,), 1)
    products_of(x + 1, 2, 2)
    rs_pass(0)
    rs_pass(1)
    products_of(x, 0, 1)
    for c in (0, 1):
        for h in (0, 1):
            zb_out[c, h] = rs_total(c, h).astype(BF16)
            if c == 0:
                z_exchange(c, h)
    for h in (0, 1):
        wait_for(s3.at[0, h], z_recv.at[0, h])
        z_exchange(1, h)
    sent(sbuf, a2a_send)

    step = half // 4

    def activate(b, c):
        def part(i, carry):
            at = pl.ds(pl.multiple_of(i * step, step), step)
            lo = zb_out[1 - c, 0, at, :].astype(F32) + s3[c, 0, at, :].astype(F32)
            hi = zb_out[1 - c, 1, at, :].astype(F32) + s3[c, 1, at, :].astype(F32)
            gate = lo[:, :ff]
            up = jnp.concatenate([lo[:, ff:], hi[:, :hf]], axis=1)
            back = hi[:, hf:]
            sig = 1.0 / (1.0 + jnp.exp(-gate))
            silu = gate * sig
            hidden = (silu * up).astype(BF16)
            g_up = (back * silu).astype(BF16)
            g_gate = (back * up * sig * (1.0 + gate * (1.0 - sig))).astype(BF16)
            ag[b, 0, at, :ff] = hidden
            ag[b, 0, at, ff:] = g_gate[:, :hf]
            ag[b, 1, at, :hf] = g_gate[:, hf:]
            ag[b, 1, at, hf:] = g_up
            return carry

        lax.fori_loop(0, 4, part, 0)

    def ag_first(c, s, g):
        mine = blk(x, s)
        for h in (g, 1 - g):
            j = 0 if g == h else 1
            sends.append(remote(ag.at[mine, g], ag.at[mine, g], ag_send.at[c, h, j],
                                ag_recv.at[c, h, j], blk(to[h], zh)))

    def ag_pass(c, s):
        for h in (0, 1):
            got = blk(come[h], s)
            wait_for(ag.at[got, h], ag_recv.at[c, h, 0])
            sends.append(remote(ag.at[got, h], ag.at[got, h], ag_send.at[c, h, 2],
                                ag_recv.at[c, h, 2], blk(to[h], zh)))

    def outputs(b):
        out = nn(ag[b, 0, :, :ff], wd[...]).astype(BF16)
        grad = nt(ag[b, 0, :, ff:], wg[:, :hf]) + nt(ag[b, 1, :, :hf], wg[:, hf:])
        grad = (grad + nt(ag[b, 1, :, hf:], wu[...])).astype(BF16)
        both = nn(put_x, out) + nn(put_y, grad)
        sbuf[pl.ds(b * ne, ne)] = both.reshape(ne, 8, wide).astype(BF16)

    def ship(b, first):
        def send(i, carry):
            o = lax.rem(i * 13, ne)
            dc, r = lax.rem(o, nc), lax.div(o, nc)
            dy, dz = lax.rem(r, ny), lax.div(r, ny)
            pex = (lax.rem(zl + dz, nzl) * ny + lax.rem(yy + dy, ny)) * nc + lax.rem(core + dc, nc)
            pltpu.make_async_remote_copy(
                src_ref=sbuf.at[b * ne + pex], dst_ref=bbuf.at[me],
                send_sem=cb_send, recv_sem=cb_recv.at[dp],
                device_id=(b, pex), device_id_type=MESH,
            ).start()
            return carry

        lax.fori_loop(first, ne, send, 0)

    def beside(s, *steps):
        def one(i, carry):
            for step in steps:
                step(blk(lax.rem(x + 1 + 2 * i, nx), s))
            return carry

        lax.fori_loop(0, 2, one, 0)

    def ship_all(b):
        ship(b, 0)

    def ag_side(c, s):
        for h in (0, 1):
            wait_for(ag.at[blk(come[h], s), 1 - h], ag_recv.at[c, h, 1])

    def ag_far(c, s):
        for h in (0, 1):
            wait_for(ag.at[blk(opposite, s), h], ag_recv.at[c, h, 2])

    activate(zpeer, 0)
    ag_first(0, 1 - zh, 0)
    ag_first(0, 1 - zh, 1)
    outputs(zpeer)
    ag_pass(0, 1 - zh)
    ag_side(0, 1 - zh)
    beside(1 - zh, outputs)
    ag_far(0, 1 - zh)
    outputs(blk(opposite, 1 - zh))
    for h in (0, 1):
        wait_for(s3.at[1, h], z_recv.at[1, h])
    ship_all(zpeer)
    activate(dp, 1)
    ag_first(1, zh, 0)
    ag_first(1, zh, 1)
    outputs(dp)
    ag_pass(1, zh)
    beside(1 - zh, ship_all)
    ship_all(blk(opposite, 1 - zh))
    ship(dp, 1)
    pltpu.make_async_copy(sbuf.at[me], bbuf.at[me], cb_recv.at[dp]).start()
    ag_side(1, zh)
    beside(zh, outputs, ship_all)
    ag_far(1, zh)
    outputs(blk(opposite, zh))
    ship_all(blk(opposite, zh))

    all_rows = nb * half

    def grads_in(m, carry):
        at = pl.ds(pl.multiple_of(m * 128, 128), 128)
        xt = xs[:, :, at].reshape(all_rows, 128)
        gwg[at, :hf] = tn(xt, ag[:, 0, :, ff:].reshape(all_rows, hf)).astype(BF16)
        rest = tn(xt, ag[:, 1, :, :].reshape(all_rows, hw))
        gwg[at, hf:] = rest[:, :hf].astype(BF16)
        gwu[at, :] = rest[:, hf:].astype(BF16)
        return carry

    lax.fori_loop(0, wide // 128, grads_in, 0)

    def grads_down(m, carry):
        at = pl.ds(pl.multiple_of(m * 128, 128), 128)
        ht = ag[:, 0, :, at].reshape(all_rows, 128)
        gwd[at, :] = tn(ht, ys[...].reshape(all_rows, wide)).astype(BF16)
        return carry

    lax.fori_loop(0, ff // 128, grads_down, 0)

    stores = [
        pltpu.make_async_copy(src, dst, out_sem.at[i])
        for i, (src, dst) in enumerate(((gwg, gwg_out), (gwu, gwu_out), (gwd, gwd_out)))
    ]
    for store in stores:
        store.start()

    here = lax.broadcasted_iota(jnp.int32, (tdev, half), 0) == pick_row
    to_grad = nn(here.astype(BF16), pick_y).astype(BF16)
    weight = jnp.where(here, gate_row, 0.0)
    w_hi = weight.astype(BF16)
    w_lo = nn((weight - w_hi.astype(F32)).astype(BF16), pick_x).astype(BF16)
    w_hi = nn(w_hi, pick_x).astype(BF16)

    def combine(i, prods):
        j = lax.rem(i, nx)
        j = j + lax.div(j, 2) * (1 - 2 * lax.rem(j, 2))
        s = lax.rem(zh + lax.div(i, nx), nzh)
        k = blk(lax.rem(x + j, nx), s)
        part = bbuf.at[pl.ds(k * ne, ne)]
        pltpu.make_async_copy(part, part, cb_recv.at[k]).wait()
        at = pl.ds(pl.multiple_of(k * wide, 128), wide)
        z = bbuf[pl.ds(k * ne, ne)].reshape(rows, wide)
        mixed[:, at] = (nn(w_hi, z) + nn(w_lo, z)).astype(BF16)
        tgrad[:, at] = nn(to_grad, z).astype(BF16)
        pltpu.make_async_copy(mixed.at[:, at], mixed_out.at[:, at], out_sem.at[3]).start()
        pltpu.make_async_copy(tgrad.at[:, at], tgrad_out.at[:, at], out_sem.at[4]).start()
        return prods + nt(cot[:, at], nn(pick_x, z).astype(BF16))

    prods = lax.fori_loop(0, nb, combine, jnp.zeros((tdev, half), F32))
    total = jnp.sum(jnp.where(here, prods, 0.0), axis=0, keepdims=True)
    top, mid, low = pieces(jnp.where(slot, total, 0.0))
    ggrad[...] = nt(top, spread) + nt(mid, spread) + nt(low, spread)
    for store in stores:
        store.wait()
    pltpu.make_async_copy(mixed, mixed_out, out_sem.at[3]).wait()
    pltpu.make_async_copy(tgrad, tgrad_out, out_sem.at[4]).wait()
    for copy in sends:
        copy.wait_send()
    sent(sbuf, cb_send)


def hand_on(*refs):
    count = (len(refs) - 2) // 3
    ins, outs, bufs = refs[:count], refs[count : 2 * count], refs[2 * count : 3 * count]
    in_sem, out_sem = refs[3 * count :]
    loads = [pltpu.make_async_copy(ins[i], bufs[i], in_sem.at[i]) for i in range(count)]
    stores = [pltpu.make_async_copy(bufs[i], outs[i], out_sem.at[i]) for i in range(count)]
    for load in loads:
        load.start()
    for load, store in zip(loads, stores):
        load.wait()
        store.start()
    for store in stores:
        store.wait()


def body(geo, tokens, cotangent, picks, gates, w_gate, w_up, w_down):
    nx, nzh, nzl, ny, nc = geo
    ne, slots = picks.shape[1], picks.shape[2]
    nb = nx * nzh
    n = nb * ne
    tdev, model = tokens.shape
    wide, ff = w_gate.shape[1], w_gate.shape[2]
    half, hw = ne * 4, 3 * ff // 2
    vm = pl.BlockSpec(memory_space=pltpu.VMEM)
    hbm = pl.BlockSpec(memory_space=pl.ANY)
    results = (
        jax.ShapeDtypeStruct((tdev, model), BF16),
        jax.ShapeDtypeStruct((tdev, model), BF16),
        jax.ShapeDtypeStruct((slots, ne), F32),
        jax.ShapeDtypeStruct((wide, ff), BF16),
        jax.ShapeDtypeStruct((wide, ff), BF16),
        jax.ShapeDtypeStruct((ff, wide), BF16),
    )
    outs = pl.pallas_call(
        functools.partial(kernel, geo),
        out_shape=results,
        in_specs=[hbm, hbm, vm, vm, hbm, hbm, hbm],
        out_specs=(hbm, hbm, vm, hbm, hbm, hbm),
        scratch_shapes=[
            pltpu.VMEM((tdev, model), BF16),
            pltpu.VMEM((tdev, model), BF16),
            pltpu.VMEM((wide, ff), BF16),
            pltpu.VMEM((wide, ff), BF16),
            pltpu.VMEM((ff, wide), BF16),
            pltpu.VMEM((tdev, model), BF16),
            pltpu.VMEM((tdev, model), BF16),
            pltpu.VMEM((wide, ff), BF16),
            pltpu.VMEM((wide, ff), BF16),
            pltpu.VMEM((ff, wide), BF16),
            pltpu.VMEM((n, 8, wide), BF16),
            pltpu.VMEM((n, 8, wide), BF16),
            pltpu.VMEM((nb, half, wide), BF16),
            pltpu.VMEM((nb, half, wide), BF16),
            pltpu.VMEM((nb, 2, half, hw), BF16),
            pltpu.VMEM((2, 2, 2, half, hw), BF16),
            pltpu.VMEM((2, 2, half, hw), BF16),
            pltpu.VMEM((2, 2, half, hw), BF16),
            pltpu.VMEM((2, 2, half, hw), BF16),
            pltpu.VMEM((2, 2, half, hw), BF16),
            pltpu.VMEM((nb, 2, half, hw), BF16),
            pltpu.VMEM((n, 8, wide), BF16),
            pltpu.SemaphoreType.DMA((5,)),
            pltpu.SemaphoreType.DMA((5,)),
            pltpu.SemaphoreType.DMA,
            pltpu.SemaphoreType.DMA((nb,)),
            pltpu.SemaphoreType.DMA((2, 2, 3)),
            pltpu.SemaphoreType.DMA((2, 2, 3)),
            pltpu.SemaphoreType.DMA((2, 2)),
            pltpu.SemaphoreType.DMA((2, 2)),
            pltpu.SemaphoreType.DMA((2, 2, 3)),
            pltpu.SemaphoreType.DMA((2, 2, 3)),
            pltpu.SemaphoreType.DMA,
            pltpu.SemaphoreType.DMA((nb,)),
        ],
        compiler_params=pltpu.CompilerParams(
            collective_id=0, has_side_effects=True, vmem_limit_bytes=62 * 1024 * 1024
        ),
        name="moe",
    )(
        tokens, cotangent, picks[0].T, gates[0].T,
        w_gate[0], w_up[0], w_down[0],
    )
    outs = pl.pallas_call(
        hand_on,
        out_shape=results,
        in_specs=[hbm] * 6,
        out_specs=(hbm,) * 6,
        scratch_shapes=[pltpu.VMEM(r.shape, r.dtype) for r in results]
        + [pltpu.SemaphoreType.DMA((6,)), pltpu.SemaphoreType.DMA((6,))],
        compiler_params=pltpu.CompilerParams(vmem_limit_bytes=62 * 1024 * 1024),
        name="hand_on",
    )(*outs)
    mixed, tgrad, ggrad, gwg, gwu, gwd = outs
    return (mixed, tgrad, ggrad.T[None], gwg[None], gwu[None], gwd[None])


def solution(mesh):
    ne = mesh.shape["expert"]
    geo = (4, 2, 4, 4, 2) if ne == 32 else (4, 2, 1, 1, ne)
    return jax.shard_map(
        functools.partial(body, geo),
        mesh=mesh,
        in_specs=(
            P(("dp", "expert"), None),
            P(("dp", "expert"), None),
            P(("dp", "expert"), None, None),
            P(("dp", "expert"), None, None),
            P("expert", "dp", None),
            P("expert", "dp", None),
            P("expert", None, "dp"),
        ),
        out_specs=(
            P(("dp", "expert"), None),
            P(("dp", "expert"), None),
            P(("dp", "expert"), None, None),
            P("expert", "dp", None),
            P("expert", "dp", None),
            P("expert", None, "dp"),
        ),
        check_vma=False,
    )
```

```python
import functools

import jax
import jax.numpy as jnp
from jax import lax
from jax.experimental import pallas as pl
from jax.experimental.pallas import tpu as pltpu
from jax.sharding import PartitionSpec as P

MESH = pl.DeviceIdType.MESH
F32 = jnp.float32
BF16 = jnp.bfloat16
GREET = 5


def nn(a, b):
    return lax.dot_general(a, b, (((1,), (0,)), ((), ())), preferred_element_type=F32)


def nt(a, b):
    return lax.dot_general(a, b, (((1,), (1,)), ((), ())), preferred_element_type=F32)


def tn(a, b):
    return lax.dot_general(a, b, (((0,), (0,)), ((), ())), preferred_element_type=F32)


def select_rows(rows, cols, shift):
    i = lax.broadcasted_iota(jnp.int32, (rows, cols), 0)
    c = lax.broadcasted_iota(jnp.int32, (rows, cols), 1)
    want = (i // 4) * 8 + i % 4 + shift
    return (want == c).astype(BF16)


def place_rows(rows, cols, shift):
    i = lax.broadcasted_iota(jnp.int32, (rows, cols), 1)
    c = lax.broadcasted_iota(jnp.int32, (rows, cols), 0)
    want = (i // 4) * 8 + i % 4 + shift
    return (want == c).astype(BF16)


def kernel(
    geo,
    tok_in, cot_in, pick_in, gate_in, wg_in, wu_in, wd_in,
    mixed_out, tgrad_out, ggrad, gwg_out, gwu_out, gwd_out,
    tok, cot, wg, wu, wd, mixed, tgrad, gwg, gwu, gwd,
    sbuf, rbuf, xs, ys, terms, s1, t1, s2, s3, zb_out, ag, bbuf,
    in_sem, out_sem, a2a_send, a2a_recv, rs_send, rs_recv, z_send, z_recv, ag_send, ag_recv,
    cb_send, cb_recv,
):
    nx, nzh, nzl, ny, nc = geo
    ne = nzl * ny * nc
    nb = nx * nzh
    n = nb * ne
    nz = nzh * nzl
    per = nz * ny * nc
    rows = ne * 8
    half = ne * 4
    tdev = tok.shape[0]
    wide = wg.shape[0]
    ff = wg.shape[1]
    hw = 3 * ff // 2
    hf = ff // 2
    dp = lax.axis_index("dp")
    ex = lax.axis_index("expert")
    me = dp * ne + ex
    x, zh = lax.div(dp, nzh), lax.rem(dp, nzh)
    core = lax.rem(ex, nc)
    yy = lax.rem(lax.div(ex, nc), ny)
    zl = lax.div(ex, nc * ny)
    zz = zh * nzl + zl

    loads = [
        pltpu.make_async_copy(src, dst, in_sem.at[i])
        for i, (src, dst) in enumerate(
            ((tok_in, tok), (cot_in, cot), (wg_in, wg), (wu_in, wu), (wd_in, wd))
        )
    ]
    barrier = pltpu.get_barrier_semaphore()
    for load in loads:
        load.start()

    def greet(i, carry):
        other = lax.rem(me + i, n)
        pl.semaphore_signal(barrier, inc=1, device_id=other, device_id_type=pl.DeviceIdType.LOGICAL)
        return carry

    lax.fori_loop(1, n, greet, 0, unroll=GREET)

    pick_x = select_rows(half, rows, 0)
    pick_y = select_rows(half, rows, 4)
    put_x = place_rows(rows, half, 0)
    put_y = place_rows(rows, half, 4)
    eye = lax.broadcasted_iota(jnp.int32, (half, half), 0) == lax.broadcasted_iota(
        jnp.int32, (half, half), 1
    )
    slot = lax.broadcasted_iota(jnp.int32, (4, half), 0) == lax.rem(
        lax.broadcasted_iota(jnp.int32, (4, half), 1), 4
    )
    spread = (
        lax.broadcasted_iota(jnp.int32, (ne, half), 0)
        == lax.div(lax.broadcasted_iota(jnp.int32, (ne, half), 1), 4)
    ).astype(BF16)

    def pieces(v):
        top = v.astype(BF16)
        rest = v - top.astype(F32)
        mid = rest.astype(BF16)
        return top, mid, (rest - mid.astype(F32)).astype(BF16)

    def in_row(v):
        top, mid, low = pieces(v)
        wide_v = nn(top, spread) + nn(mid, spread) + nn(low, spread)
        return jnp.sum(jnp.where(slot, wide_v, 0.0), axis=0, keepdims=True)

    pick_row = in_row(pick_in[...].astype(F32)).astype(jnp.int32)
    gate_row = in_row(gate_in[...])
    pick_col = jnp.sum(jnp.where(eye, pick_row, 0), axis=1, keepdims=True)
    gate_col = jnp.sum(jnp.where(eye, gate_row, 0.0), axis=1, keepdims=True)
    hot = (lax.broadcasted_iota(jnp.int32, (half, tdev), 1) == pick_col).astype(BF16)

    def gather(k, carry):
        at = pl.ds(pl.multiple_of(k * wide, 128), wide)
        token_rows = nn(hot, tok[:, at]).astype(BF16)
        grad_rows = (nn(hot, cot[:, at]) * gate_col).astype(BF16)
        both = nn(put_x, token_rows) + nn(put_y, grad_rows)
        sbuf[pl.ds(k * ne, ne)] = both.reshape(ne, 8, wide).astype(BF16)
        return carry

    loads[0].wait()
    loads[1].wait()
    lax.fori_loop(0, nb, gather, 0)
    pl.semaphore_wait(barrier, n - 1)

    def dispatch(ways, first):
        def send(i, carry):
            dx = ways[0]
            if len(ways) == 2:
                dx = ways[0] + (ways[1] - ways[0]) * lax.rem(i, 2)
            o = lax.rem(lax.div(i, len(ways)) * 37, per)
            dc, r = lax.rem(o, nc), lax.div(o, nc)
            dz, dy = lax.rem(r, nz), lax.div(r, nz)
            pz = lax.rem(zz + dz, nz)
            pdp = lax.rem(x + dx, nx) * nzh + lax.div(pz, nzl)
            pex = (lax.rem(pz, nzl) * ny + lax.rem(yy + dy, ny)) * nc + lax.rem(core + dc, nc)
            pltpu.make_async_remote_copy(
                src_ref=sbuf.at[pdp * ne + pex], dst_ref=rbuf.at[me],
                send_sem=a2a_send, recv_sem=a2a_recv.at[dp],
                device_id=(pdp, pex), device_id_type=MESH,
            ).start()
            return carry

        lax.fori_loop(first, per * len(ways), send, 0)

    dispatch((2,), 0)
    dispatch((1, 3), 0)
    dispatch((0,), 1)
    pltpu.make_async_copy(sbuf.at[me], rbuf.at[me], a2a_recv.at[dp]).start()

    def sent(src, send_sem):
        part = src.at[pl.ds(0, n - 1)]
        pltpu.make_async_copy(part, part, send_sem).wait()

    def products(b):
        part = rbuf.at[pl.ds(b * ne, ne)]
        pltpu.make_async_copy(part, part, a2a_recv.at[b]).wait()
        z = rbuf[pl.ds(b * ne, ne)].reshape(rows, wide)
        xb = nn(pick_x, z).astype(BF16)
        yb = nn(pick_y, z).astype(BF16)
        xs[b] = xb
        ys[b] = yb
        terms[b, 0, :, :ff] = nn(xb, wg[...]).astype(BF16)
        up = nn(xb, wu[...]).astype(BF16)
        terms[b, 0, :, ff:] = up[:, :hf]
        terms[b, 1, :, :hf] = up[:, hf:]
        terms[b, 1, :, hf:] = nt(yb, wd[...]).astype(BF16)

    to = (lax.rem(x + 1, nx), lax.rem(x + nx - 1, nx))
    come = (to[1], to[0])
    opposite = lax.rem(x + 2, nx)
    side = (zh, 1 - zh)

    def blk(q, s):
        return q * nzh + s

    def remote(src, dst, send_sem, recv_sem, pdp):
        copy = pltpu.make_async_remote_copy(
            src_ref=src, dst_ref=dst, send_sem=send_sem, recv_sem=recv_sem,
            device_id=(pdp, ex), device_id_type=MESH,
        )
        copy.start()
        return copy

    def wait_for(dst, sem):
        pltpu.make_async_copy(dst, dst, sem).wait()

    sends = []

    def rs_first(c):
        for h in (0, 1):
            sends.append(remote(terms.at[blk(opposite, side[c]), h], s1.at[c, h, 1],
                                rs_send.at[c, h, 0], rs_recv.at[c, h, 0], blk(to[h], zh)))

    def rs_pass(c):
        for h in (0, 1):
            sends.append(remote(terms.at[blk(to[h], side[c]), 1 - h], s1.at[c, 1 - h, 0],
                                rs_send.at[c, h, 1], rs_recv.at[c, 1 - h, 1], blk(to[h], zh)))
        for h in (0, 1):
            wait_for(s1.at[c, h, 1], rs_recv.at[c, h, 0])
            t1[c, h] = (terms[blk(to[h], side[c]), h].astype(F32) + s1[c, h, 1].astype(F32)).astype(BF16)
            sends.append(remote(t1.at[c, h], s2.at[c, h], rs_send.at[c, h, 2], rs_recv.at[c, h, 2],
                                blk(to[h], zh)))

    def rs_total(c, h):
        wait_for(s1.at[c, h, 0], rs_recv.at[c, h, 1])
        wait_for(s2.at[c, h], rs_recv.at[c, h, 2])
        return (terms[blk(x, side[c]), h].astype(F32) + s1[c, h, 0].astype(F32)
                + s2[c, h].astype(F32))

    def products_of(first, gap, count, s):
        def one(i, carry):
            products(blk(lax.rem(first + gap * i, nx), s))
            return carry

        lax.fori_loop(0, count, one, 0)

    zpeer = blk(x, 1 - zh)

    def z_exchange(c, h):
        sends.append(remote(zb_out.at[c, h], s3.at[c, h], z_send.at[c, h], z_recv.at[c, h], zpeer))

    for load in loads[2:]:
        load.wait()
    for c in (0, 1):
        products_of(opposite, 0, 1, side[c])
        rs_first(c)
    for c in (0, 1):
        products_of(x + 1, 2, 2, side[c])
        rs_pass(c)
    for c in (0, 1):
        products_of(x, 0, 1, side[c])
        for h in (0, 1):
            zb_out[c, h] = rs_total(c, h).astype(BF16)
            if c == 0:
                z_exchange(c, h)
    for h in (0, 1):
        wait_for(s3.at[0, h], z_recv.at[0, h])
        z_exchange(1, h)
    sent(sbuf, a2a_send)

    step = half // 4

    def activate(b, c):
        def part(i, carry):
            at = pl.ds(pl.multiple_of(i * step, step), step)
            lo = zb_out[1 - c, 0, at, :].astype(F32) + s3[c, 0, at, :].astype(F32)
            hi = zb_out[1 - c, 1, at, :].astype(F32) + s3[c, 1, at, :].astype(F32)
            gate = lo[:, :ff]
            up = jnp.concatenate([lo[:, ff:], hi[:, :hf]], axis=1)
            back = hi[:, hf:]
            sig = 1.0 / (1.0 + jnp.exp(-gate))
            silu = gate * sig
            hidden = (silu * up).astype(BF16)
            g_up = (back * silu).astype(BF16)
            g_gate = (back * up * sig * (1.0 + gate * (1.0 - sig))).astype(BF16)
            ag[b, 0, at, :ff] = hidden
            ag[b, 0, at, ff:] = g_gate[:, :hf]
            ag[b, 1, at, :hf] = g_gate[:, hf:]
            ag[b, 1, at, hf:] = g_up
            return carry

        lax.fori_loop(0, 4, part, 0)

    def ag_first(c, s, g):
        mine = blk(x, s)
        for h in (g, 1 - g):
            j = 0 if g == h else 1
            sends.append(remote(ag.at[mine, g], ag.at[mine, g], ag_send.at[c, h, j],
                                ag_recv.at[c, h, j], blk(to[h], zh)))

    def ag_pass(c, s):
        for h in (0, 1):
            got = blk(come[h], s)
            wait_for(ag.at[got, h], ag_recv.at[c, h, 0])
            sends.append(remote(ag.at[got, h], ag.at[got, h], ag_send.at[c, h, 2],
                                ag_recv.at[c, h, 2], blk(to[h], zh)))

    def outputs(b):
        out = nn(ag[b, 0, :, :ff], wd[...]).astype(BF16)
        grad = nt(ag[b, 0, :, ff:], wg[:, :hf]) + nt(ag[b, 1, :, :hf], wg[:, hf:])
        grad = (grad + nt(ag[b, 1, :, hf:], wu[...])).astype(BF16)
        both = nn(put_x, out) + nn(put_y, grad)
        sbuf[pl.ds(b * ne, ne)] = both.reshape(ne, 8, wide).astype(BF16)

    def ship(b, first):
        def send(i, carry):
            o = lax.rem(i * 13, ne)
            dc, r = lax.rem(o, nc), lax.div(o, nc)
            dy, dz = lax.rem(r, ny), lax.div(r, ny)
            pex = (lax.rem(zl + dz, nzl) * ny + lax.rem(yy + dy, ny)) * nc + lax.rem(core + dc, nc)
            pltpu.make_async_remote_copy(
                src_ref=sbuf.at[b * ne + pex], dst_ref=bbuf.at[me],
                send_sem=cb_send, recv_sem=cb_recv.at[dp],
                device_id=(b, pex), device_id_type=MESH,
            ).start()
            return carry

        lax.fori_loop(first, ne, send, 0)

    def beside(s, *steps):
        def one(i, carry):
            for step in steps:
                step(blk(lax.rem(x + 1 + 2 * i, nx), s))
            return carry

        lax.fori_loop(0, 2, one, 0)

    def ship_all(b):
        ship(b, 0)

    def ag_side(c, s):
        for h in (0, 1):
            wait_for(ag.at[blk(come[h], s), 1 - h], ag_recv.at[c, h, 1])

    def ag_far(c, s):
        for h in (0, 1):
            wait_for(ag.at[blk(opposite, s), h], ag_recv.at[c, h, 2])

    activate(zpeer, 0)
    ag_first(0, 1 - zh, 0)
    ag_first(0, 1 - zh, 1)
    outputs(zpeer)
    ag_pass(0, 1 - zh)
    ag_side(0, 1 - zh)
    beside(1 - zh, outputs)
    ag_far(0, 1 - zh)
    outputs(blk(opposite, 1 - zh))
    wait_for(s3.at[1, 0], z_recv.at[1, 0])
    ship_all(zpeer)
    wait_for(s3.at[1, 1], z_recv.at[1, 1])
    activate(dp, 1)
    ag_first(1, zh, 0)
    ag_first(1, zh, 1)
    beside(1 - zh, ship_all)
    ship_all(blk(opposite, 1 - zh))
    outputs(dp)
    ship(dp, 1)
    pltpu.make_async_copy(sbuf.at[me], bbuf.at[me], cb_recv.at[dp]).start()
    ag_pass(1, zh)
    ag_side(1, zh)
    beside(zh, outputs, ship_all)
    ag_far(1, zh)
    outputs(blk(opposite, zh))
    ship_all(blk(opposite, zh))

    all_rows = nb * half

    def grads_in(m, carry):
        at = pl.ds(pl.multiple_of(m * 128, 128), 128)
        xt = xs[:, :, at].reshape(all_rows, 128)
        gwg[at, :hf] = tn(xt, ag[:, 0, :, ff:].reshape(all_rows, hf)).astype(BF16)
        rest = tn(xt, ag[:, 1, :, :].reshape(all_rows, hw))
        gwg[at, hf:] = rest[:, :hf].astype(BF16)
        gwu[at, :] = rest[:, hf:].astype(BF16)
        return carry

    lax.fori_loop(0, wide // 128, grads_in, 0)

    def grads_down(m, carry):
        at = pl.ds(pl.multiple_of(m * 128, 128), 128)
        ht = ag[:, 0, :, at].reshape(all_rows, 128)
        gwd[at, :] = tn(ht, ys[...].reshape(all_rows, wide)).astype(BF16)
        return carry

    lax.fori_loop(0, ff // 128, grads_down, 0)

    stores = [
        pltpu.make_async_copy(src, dst, out_sem.at[i])
        for i, (src, dst) in enumerate(((gwg, gwg_out), (gwu, gwu_out), (gwd, gwd_out)))
    ]
    for store in stores:
        store.start()

    here = lax.broadcasted_iota(jnp.int32, (tdev, half), 0) == pick_row
    to_grad = nn(here.astype(BF16), pick_y).astype(BF16)
    weight = jnp.where(here, gate_row, 0.0)
    w_hi = weight.astype(BF16)
    w_lo = nn((weight - w_hi.astype(F32)).astype(BF16), pick_x).astype(BF16)
    w_hi = nn(w_hi, pick_x).astype(BF16)

    def combine(i, prods):
        j = lax.rem(i, nx)
        j = j + lax.div(j, 2) * (1 - 2 * lax.rem(j, 2))
        s = lax.rem(zh + lax.div(i, nx), nzh)
        k = blk(lax.rem(x + j, nx), s)
        part = bbuf.at[pl.ds(k * ne, ne)]
        pltpu.make_async_copy(part, part, cb_recv.at[k]).wait()
        at = pl.ds(pl.multiple_of(k * wide, 128), wide)
        z = bbuf[pl.ds(k * ne, ne)].reshape(rows, wide)
        mixed[:, at] = (nn(w_hi, z) + nn(w_lo, z)).astype(BF16)
        tgrad[:, at] = nn(to_grad, z).astype(BF16)
        pltpu.make_async_copy(mixed.at[:, at], mixed_out.at[:, at], out_sem.at[3]).start()
        pltpu.make_async_copy(tgrad.at[:, at], tgrad_out.at[:, at], out_sem.at[4]).start()
        return prods + nt(cot[:, at], nn(pick_x, z).astype(BF16))

    prods = lax.fori_loop(0, nb, combine, jnp.zeros((tdev, half), F32))
    total = jnp.sum(jnp.where(here, prods, 0.0), axis=0, keepdims=True)
    top, mid, low = pieces(jnp.where(slot, total, 0.0))
    ggrad[...] = nt(top, spread) + nt(mid, spread) + nt(low, spread)
    for store in stores:
        store.wait()
    pltpu.make_async_copy(mixed, mixed_out, out_sem.at[3]).wait()
    pltpu.make_async_copy(tgrad, tgrad_out, out_sem.at[4]).wait()
    for copy in sends:
        copy.wait_send()
    sent(sbuf, cb_send)


def hand_on(*refs):
    count = (len(refs) - 1) // 2
    copies = [
        pltpu.make_async_copy(refs[i], refs[count + i], refs[-1].at[i]) for i in range(count)
    ]
    for copy in copies:
        copy.start()
    for copy in copies:
        copy.wait()


def body(geo, tokens, cotangent, picks, gates, w_gate, w_up, w_down):
    nx, nzh, nzl, ny, nc = geo
    ne, slots = picks.shape[1], picks.shape[2]
    nb = nx * nzh
    n = nb * ne
    tdev, model = tokens.shape
    wide, ff = w_gate.shape[1], w_gate.shape[2]
    half, hw = ne * 4, 3 * ff // 2
    vm = pl.BlockSpec(memory_space=pltpu.VMEM)
    hbm = pl.BlockSpec(memory_space=pl.ANY)
    far = pl.BlockSpec(memory_space=pltpu.HBM)
    results = (
        jax.ShapeDtypeStruct((tdev, model), BF16),
        jax.ShapeDtypeStruct((tdev, model), BF16),
        jax.ShapeDtypeStruct((slots, ne), F32),
        jax.ShapeDtypeStruct((wide, ff), BF16),
        jax.ShapeDtypeStruct((wide, ff), BF16),
        jax.ShapeDtypeStruct((ff, wide), BF16),
    )
    outs = pl.pallas_call(
        functools.partial(kernel, geo),
        out_shape=results,
        in_specs=[far, far, vm, vm, far, far, far],
        out_specs=(hbm, hbm, vm, hbm, hbm, hbm),
        scratch_shapes=[
            pltpu.VMEM((tdev, model), BF16),
            pltpu.VMEM((tdev, model), BF16),
            pltpu.VMEM((wide, ff), BF16),
            pltpu.VMEM((wide, ff), BF16),
            pltpu.VMEM((ff, wide), BF16),
            pltpu.VMEM((tdev, model), BF16),
            pltpu.VMEM((tdev, model), BF16),
            pltpu.VMEM((wide, ff), BF16),
            pltpu.VMEM((wide, ff), BF16),
            pltpu.VMEM((ff, wide), BF16),
            pltpu.VMEM((n, 8, wide), BF16),
            pltpu.VMEM((n, 8, wide), BF16),
            pltpu.VMEM((nb, half, wide), BF16),
            pltpu.VMEM((nb, half, wide), BF16),
            pltpu.VMEM((nb, 2, half, hw), BF16),
            pltpu.VMEM((2, 2, 2, half, hw), BF16),
            pltpu.VMEM((2, 2, half, hw), BF16),
            pltpu.VMEM((2, 2, half, hw), BF16),
            pltpu.VMEM((2, 2, half, hw), BF16),
            pltpu.VMEM((2, 2, half, hw), BF16),
            pltpu.VMEM((nb, 2, half, hw), BF16),
            pltpu.VMEM((n, 8, wide), BF16),
            pltpu.SemaphoreType.DMA((5,)),
            pltpu.SemaphoreType.DMA((5,)),
            pltpu.SemaphoreType.DMA,
            pltpu.SemaphoreType.DMA((nb,)),
            pltpu.SemaphoreType.DMA((2, 2, 3)),
            pltpu.SemaphoreType.DMA((2, 2, 3)),
            pltpu.SemaphoreType.DMA((2, 2)),
            pltpu.SemaphoreType.DMA((2, 2)),
            pltpu.SemaphoreType.DMA((2, 2, 3)),
            pltpu.SemaphoreType.DMA((2, 2, 3)),
            pltpu.SemaphoreType.DMA,
            pltpu.SemaphoreType.DMA((nb,)),
        ],
        compiler_params=pltpu.CompilerParams(
            collective_id=0, has_side_effects=True, vmem_limit_bytes=46 * 1024 * 1024
        ),
        name="moe",
    )(
        *(
            pltpu.with_memory_space_constraint(v, pltpu.HBM)
            for v in (tokens, cotangent, picks[0].T, gates[0].T, w_gate[0], w_up[0], w_down[0])
        ),
    )
    outs = pl.pallas_call(
        hand_on,
        out_shape=results,
        in_specs=[hbm] * 6,
        out_specs=(hbm,) * 6,
        scratch_shapes=[pltpu.SemaphoreType.DMA((6,))],
        compiler_params=pltpu.CompilerParams(vmem_limit_bytes=12 * 1024 * 1024),
        name="hand_on",
    )(*outs)
    mixed, tgrad, ggrad, gwg, gwu, gwd = outs
    return (mixed, tgrad, ggrad.T[None], gwg[None], gwu[None], gwd[None])


def solution(mesh):
    ne = mesh.shape["expert"]
    geo = (4, 2, 4, 4, 2) if ne == 32 else (4, 2, 1, 1, ne)
    return jax.shard_map(
        functools.partial(body, geo),
        mesh=mesh,
        in_specs=(
            P(("dp", "expert"), None),
            P(("dp", "expert"), None),
            P(("dp", "expert"), None, None),
            P(("dp", "expert"), None, None),
            P("expert", "dp", None),
            P("expert", "dp", None),
            P("expert", None, "dp"),
        ),
        out_specs=(
            P(("dp", "expert"), None),
            P(("dp", "expert"), None),
            P(("dp", "expert"), None, None),
            P("expert", "dp", None),
            P("expert", "dp", None),
            P("expert", None, "dp"),
        ),
        check_vma=False,
    )
```

```python
import functools

import jax
import jax.numpy as jnp
from jax import lax
from jax.experimental import pallas as pl
from jax.experimental.pallas import tpu as pltpu
from jax.sharding import PartitionSpec as P

MESH = pl.DeviceIdType.MESH
F32 = jnp.float32
BF16 = jnp.bfloat16
GREET = 5


def nn(a, b):
    return lax.dot_general(a, b, (((1,), (0,)), ((), ())), preferred_element_type=F32)


def nt(a, b):
    return lax.dot_general(a, b, (((1,), (1,)), ((), ())), preferred_element_type=F32)


def tn(a, b):
    return lax.dot_general(a, b, (((0,), (0,)), ((), ())), preferred_element_type=F32)


def select_rows(rows, cols, shift):
    i = lax.broadcasted_iota(jnp.int32, (rows, cols), 0)
    c = lax.broadcasted_iota(jnp.int32, (rows, cols), 1)
    want = (i // 4) * 8 + i % 4 + shift
    return (want == c).astype(BF16)


def place_rows(rows, cols, shift):
    i = lax.broadcasted_iota(jnp.int32, (rows, cols), 1)
    c = lax.broadcasted_iota(jnp.int32, (rows, cols), 0)
    want = (i // 4) * 8 + i % 4 + shift
    return (want == c).astype(BF16)


def kernel(
    geo,
    tok_in, cot_in, pick_in, gate_in, wg_in, wu_in, wd_in,
    mixed_out, tgrad_out, ggrad, gwg_out, gwu_out, gwd_out,
    tok, cot, wg, wu, wd, mixed, tgrad, gwg, gwu, gwd,
    sbuf, rbuf, xs, ys, terms, s1, t1, s2, s3, zb_out, ag, bbuf,
    in_sem, out_sem, a2a_send, a2a_recv, rs_send, rs_recv, z_send, z_recv, ag_send, ag_recv,
    cb_send, cb_recv,
):
    nx, nzh, nzl, ny, nc = geo
    ne = nzl * ny * nc
    nb = nx * nzh
    n = nb * ne
    nz = nzh * nzl
    per = nz * ny * nc
    rows = ne * 8
    half = ne * 4
    tdev = tok.shape[0]
    wide = wg.shape[0]
    ff = wg.shape[1]
    hw = 3 * ff // 2
    hf = ff // 2
    dp = lax.axis_index("dp")
    ex = lax.axis_index("expert")
    me = dp * ne + ex
    x, zh = lax.div(dp, nzh), lax.rem(dp, nzh)
    core = lax.rem(ex, nc)
    yy = lax.rem(lax.div(ex, nc), ny)
    zl = lax.div(ex, nc * ny)
    zz = zh * nzl + zl

    loads = [
        pltpu.make_async_copy(src, dst, in_sem.at[i])
        for i, (src, dst) in enumerate(
            ((tok_in, tok), (cot_in, cot), (wg_in, wg), (wu_in, wu), (wd_in, wd))
        )
    ]
    barrier = pltpu.get_barrier_semaphore()
    for load in loads:
        load.start()

    def greet(i, carry):
        other = lax.rem(me + i, n)
        pl.semaphore_signal(barrier, inc=1, device_id=other, device_id_type=pl.DeviceIdType.LOGICAL)
        return carry

    lax.fori_loop(1, n, greet, 0, unroll=GREET)

    pick_x = select_rows(half, rows, 0)
    pick_y = select_rows(half, rows, 4)
    put_x = place_rows(rows, half, 0)
    put_y = place_rows(rows, half, 4)
    eye = lax.broadcasted_iota(jnp.int32, (half, half), 0) == lax.broadcasted_iota(
        jnp.int32, (half, half), 1
    )
    slot = lax.broadcasted_iota(jnp.int32, (4, half), 0) == lax.rem(
        lax.broadcasted_iota(jnp.int32, (4, half), 1), 4
    )
    spread = (
        lax.broadcasted_iota(jnp.int32, (ne, half), 0)
        == lax.div(lax.broadcasted_iota(jnp.int32, (ne, half), 1), 4)
    ).astype(BF16)

    def pieces(v):
        top = v.astype(BF16)
        rest = v - top.astype(F32)
        mid = rest.astype(BF16)
        return top, mid, (rest - mid.astype(F32)).astype(BF16)

    def in_row(v):
        top, mid, low = pieces(v)
        wide_v = nn(top, spread) + nn(mid, spread) + nn(low, spread)
        return jnp.sum(jnp.where(slot, wide_v, 0.0), axis=0, keepdims=True)

    pick_row = in_row(pick_in[...].astype(F32)).astype(jnp.int32)
    gate_row = in_row(gate_in[...])
    pick_col = jnp.sum(jnp.where(eye, pick_row, 0), axis=1, keepdims=True)
    gate_col = jnp.sum(jnp.where(eye, gate_row, 0.0), axis=1, keepdims=True)
    hot = (lax.broadcasted_iota(jnp.int32, (half, tdev), 1) == pick_col).astype(BF16)

    def gather(k, carry):
        at = pl.ds(pl.multiple_of(k * wide, 128), wide)
        token_rows = nn(hot, tok[:, at]).astype(BF16)
        grad_rows = (nn(hot, cot[:, at]) * gate_col).astype(BF16)
        both = nn(put_x, token_rows) + nn(put_y, grad_rows)
        sbuf[pl.ds(k * ne, ne)] = both.reshape(ne, 8, wide).astype(BF16)
        return carry

    loads[0].wait()
    loads[1].wait()
    lax.fori_loop(0, nb, gather, 0)
    pl.semaphore_wait(barrier, n - 1)

    def dispatch(ways, first):
        def send(i, carry):
            dx = ways[0]
            if len(ways) == 2:
                dx = ways[0] + (ways[1] - ways[0]) * lax.rem(i, 2)
            o = lax.rem(lax.div(i, len(ways)) * 37, per)
            dc, r = lax.rem(o, nc), lax.div(o, nc)
            dz, dy = lax.rem(r, nz), lax.div(r, nz)
            pz = lax.rem(zz + dz, nz)
            pdp = lax.rem(x + dx, nx) * nzh + lax.div(pz, nzl)
            pex = (lax.rem(pz, nzl) * ny + lax.rem(yy + dy, ny)) * nc + lax.rem(core + dc, nc)
            pltpu.make_async_remote_copy(
                src_ref=sbuf.at[pdp * ne + pex], dst_ref=rbuf.at[me],
                send_sem=a2a_send, recv_sem=a2a_recv.at[dp],
                device_id=(pdp, pex), device_id_type=MESH,
            ).start()
            return carry

        lax.fori_loop(first, per * len(ways), send, 0)

    dispatch((2,), 0)
    dispatch((1, 3), 0)
    dispatch((0,), 1)
    pltpu.make_async_copy(sbuf.at[me], rbuf.at[me], a2a_recv.at[dp]).start()

    def sent(src, send_sem):
        part = src.at[pl.ds(0, n - 1)]
        pltpu.make_async_copy(part, part, send_sem).wait()

    def products(b):
        part = rbuf.at[pl.ds(b * ne, ne)]
        pltpu.make_async_copy(part, part, a2a_recv.at[b]).wait()
        z = rbuf[pl.ds(b * ne, ne)].reshape(rows, wide)
        xb = nn(pick_x, z).astype(BF16)
        yb = nn(pick_y, z).astype(BF16)
        xs[b] = xb
        ys[b] = yb
        terms[b, 0, :, :ff] = nn(xb, wg[...]).astype(BF16)
        up = nn(xb, wu[...]).astype(BF16)
        terms[b, 0, :, ff:] = up[:, :hf]
        terms[b, 1, :, :hf] = up[:, hf:]
        terms[b, 1, :, hf:] = nt(yb, wd[...]).astype(BF16)

    to = (lax.rem(x + 1, nx), lax.rem(x + nx - 1, nx))
    come = (to[1], to[0])
    opposite = lax.rem(x + 2, nx)
    side = (zh, 1 - zh)

    def blk(q, s):
        return q * nzh + s

    def remote(src, dst, send_sem, recv_sem, pdp):
        copy = pltpu.make_async_remote_copy(
            src_ref=src, dst_ref=dst, send_sem=send_sem, recv_sem=recv_sem,
            device_id=(pdp, ex), device_id_type=MESH,
        )
        copy.start()
        return copy

    def wait_for(dst, sem):
        pltpu.make_async_copy(dst, dst, sem).wait()

    sends = []

    def rs_first(c):
        for h in (0, 1):
            sends.append(remote(terms.at[blk(opposite, side[c]), h], s1.at[c, h, 1],
                                rs_send.at[c, h, 0], rs_recv.at[c, h, 0], blk(to[h], zh)))

    def rs_pass(c):
        for h in (0, 1):
            sends.append(remote(terms.at[blk(to[h], side[c]), 1 - h], s1.at[c, 1 - h, 0],
                                rs_send.at[c, h, 1], rs_recv.at[c, 1 - h, 1], blk(to[h], zh)))
        for h in (0, 1):
            wait_for(s1.at[c, h, 1], rs_recv.at[c, h, 0])
            t1[c, h] = (terms[blk(to[h], side[c]), h].astype(F32) + s1[c, h, 1].astype(F32)).astype(BF16)
            sends.append(remote(t1.at[c, h], s2.at[c, h], rs_send.at[c, h, 2], rs_recv.at[c, h, 2],
                                blk(to[h], zh)))

    def rs_total(c, h):
        wait_for(s1.at[c, h, 0], rs_recv.at[c, h, 1])
        wait_for(s2.at[c, h], rs_recv.at[c, h, 2])
        return (terms[blk(x, side[c]), h].astype(F32) + s1[c, h, 0].astype(F32)
                + s2[c, h].astype(F32))

    def products_of(first, gap, count, s):
        def one(i, carry):
            products(blk(lax.rem(first + gap * i, nx), s))
            return carry

        lax.fori_loop(0, count, one, 0)

    zpeer = blk(x, 1 - zh)

    def z_exchange(c, h):
        sends.append(remote(zb_out.at[c, h], s3.at[c, h], z_send.at[c, h], z_recv.at[c, h], zpeer))

    for load in loads[2:]:
        load.wait()
    for c in (0, 1):
        products_of(opposite, 0, 1, side[c])
        rs_first(c)
    for c in (0, 1):
        products_of(x + 1, 2, 2, side[c])
        rs_pass(c)
    for c in (0, 1):
        products_of(x, 0, 1, side[c])
        for h in (0, 1):
            zb_out[c, h] = rs_total(c, h).astype(BF16)
            if c == 0 or h == 0:
                z_exchange(c, h)
    wait_for(s3.at[0, 0], z_recv.at[0, 0])
    z_exchange(1, 1)
    wait_for(s3.at[0, 1], z_recv.at[0, 1])
    sent(sbuf, a2a_send)

    step = half // 4

    def activate(b, c):
        def part(i, carry):
            at = pl.ds(pl.multiple_of(i * step, step), step)
            lo = zb_out[1 - c, 0, at, :].astype(F32) + s3[c, 0, at, :].astype(F32)
            hi = zb_out[1 - c, 1, at, :].astype(F32) + s3[c, 1, at, :].astype(F32)
            gate = lo[:, :ff]
            up = jnp.concatenate([lo[:, ff:], hi[:, :hf]], axis=1)
            back = hi[:, hf:]
            sig = 1.0 / (1.0 + jnp.exp(-gate))
            silu = gate * sig
            hidden = (silu * up).astype(BF16)
            g_up = (back * silu).astype(BF16)
            g_gate = (back * up * sig * (1.0 + gate * (1.0 - sig))).astype(BF16)
            ag[b, 0, at, :ff] = hidden
            ag[b, 0, at, ff:] = g_gate[:, :hf]
            ag[b, 1, at, :hf] = g_gate[:, hf:]
            ag[b, 1, at, hf:] = g_up
            return carry

        lax.fori_loop(0, 4, part, 0)

    def ag_first(c, s, g):
        mine = blk(x, s)
        for h in (g, 1 - g):
            j = 0 if g == h else 1
            sends.append(remote(ag.at[mine, g], ag.at[mine, g], ag_send.at[c, h, j],
                                ag_recv.at[c, h, j], blk(to[h], zh)))

    def ag_pass(c, s):
        for h in (0, 1):
            got = blk(come[h], s)
            wait_for(ag.at[got, h], ag_recv.at[c, h, 0])
            sends.append(remote(ag.at[got, h], ag.at[got, h], ag_send.at[c, h, 2],
                                ag_recv.at[c, h, 2], blk(to[h], zh)))

    def outputs(b):
        out = nn(ag[b, 0, :, :ff], wd[...]).astype(BF16)
        grad = nt(ag[b, 0, :, ff:], wg[:, :hf]) + nt(ag[b, 1, :, :hf], wg[:, hf:])
        grad = (grad + nt(ag[b, 1, :, hf:], wu[...])).astype(BF16)
        both = nn(put_x, out) + nn(put_y, grad)
        sbuf[pl.ds(b * ne, ne)] = both.reshape(ne, 8, wide).astype(BF16)

    def ship(b, first):
        def send(i, carry):
            o = lax.rem(i * 13, ne)
            dc, r = lax.rem(o, nc), lax.div(o, nc)
            dy, dz = lax.rem(r, ny), lax.div(r, ny)
            pex = (lax.rem(zl + dz, nzl) * ny + lax.rem(yy + dy, ny)) * nc + lax.rem(core + dc, nc)
            pltpu.make_async_remote_copy(
                src_ref=sbuf.at[b * ne + pex], dst_ref=bbuf.at[me],
                send_sem=cb_send, recv_sem=cb_recv.at[dp],
                device_id=(b, pex), device_id_type=MESH,
            ).start()
            return carry

        lax.fori_loop(first, ne, send, 0)

    def beside(s, *steps):
        def one(i, carry):
            for step in steps:
                step(blk(lax.rem(x + 1 + 2 * i, nx), s))
            return carry

        lax.fori_loop(0, 2, one, 0)

    def ship_all(b):
        ship(b, 0)

    def ag_side(c, s):
        for h in (0, 1):
            wait_for(ag.at[blk(come[h], s), 1 - h], ag_recv.at[c, h, 1])

    def ag_far(c, s):
        for h in (0, 1):
            wait_for(ag.at[blk(opposite, s), h], ag_recv.at[c, h, 2])

    activate(zpeer, 0)
    ag_first(0, 1 - zh, 0)
    ag_first(0, 1 - zh, 1)
    outputs(zpeer)
    ag_pass(0, 1 - zh)
    ag_side(0, 1 - zh)
    beside(1 - zh, outputs)
    ag_far(0, 1 - zh)
    outputs(blk(opposite, 1 - zh))
    wait_for(s3.at[1, 0], z_recv.at[1, 0])
    ship_all(zpeer)
    wait_for(s3.at[1, 1], z_recv.at[1, 1])
    activate(dp, 1)
    ag_first(1, zh, 0)
    ag_first(1, zh, 1)
    beside(1 - zh, ship_all)
    ship_all(blk(opposite, 1 - zh))
    outputs(dp)
    ship(dp, 1)
    pltpu.make_async_copy(sbuf.at[me], bbuf.at[me], cb_recv.at[dp]).start()
    ag_pass(1, zh)
    ag_side(1, zh)
    beside(zh, outputs, ship_all)
    ag_far(1, zh)
    outputs(blk(opposite, zh))
    ship_all(blk(opposite, zh))

    all_rows = nb * half

    def grads_in(m, carry):
        at = pl.ds(pl.multiple_of(m * 128, 128), 128)
        xt = xs[:, :, at].reshape(all_rows, 128)
        gwg[at, :hf] = tn(xt, ag[:, 0, :, ff:].reshape(all_rows, hf)).astype(BF16)
        rest = tn(xt, ag[:, 1, :, :].reshape(all_rows, hw))
        gwg[at, hf:] = rest[:, :hf].astype(BF16)
        gwu[at, :] = rest[:, hf:].astype(BF16)
        return carry

    lax.fori_loop(0, wide // 128, grads_in, 0)

    def grads_down(m, carry):
        at = pl.ds(pl.multiple_of(m * 128, 128), 128)
        ht = ag[:, 0, :, at].reshape(all_rows, 128)
        gwd[at, :] = tn(ht, ys[...].reshape(all_rows, wide)).astype(BF16)
        return carry

    lax.fori_loop(0, ff // 128, grads_down, 0)

    stores = [
        pltpu.make_async_copy(src, dst, out_sem.at[i])
        for i, (src, dst) in enumerate(((gwg, gwg_out), (gwu, gwu_out), (gwd, gwd_out)))
    ]
    for store in stores:
        store.start()

    here = lax.broadcasted_iota(jnp.int32, (tdev, half), 0) == pick_row
    to_grad = nn(here.astype(BF16), pick_y).astype(BF16)
    weight = jnp.where(here, gate_row, 0.0)
    w_hi = weight.astype(BF16)
    w_lo = nn((weight - w_hi.astype(F32)).astype(BF16), pick_x).astype(BF16)
    w_hi = nn(w_hi, pick_x).astype(BF16)

    def combine(i, prods):
        j = lax.rem(i, nx)
        j = j + lax.div(j, 2) * (1 - 2 * lax.rem(j, 2))
        s = lax.rem(zh + lax.div(i, nx), nzh)
        k = blk(lax.rem(x + j, nx), s)
        part = bbuf.at[pl.ds(k * ne, ne)]
        pltpu.make_async_copy(part, part, cb_recv.at[k]).wait()
        at = pl.ds(pl.multiple_of(k * wide, 128), wide)
        z = bbuf[pl.ds(k * ne, ne)].reshape(rows, wide)
        mixed[:, at] = (nn(w_hi, z) + nn(w_lo, z)).astype(BF16)
        tgrad[:, at] = nn(to_grad, z).astype(BF16)
        pltpu.make_async_copy(mixed.at[:, at], mixed_out.at[:, at], out_sem.at[3]).start()
        pltpu.make_async_copy(tgrad.at[:, at], tgrad_out.at[:, at], out_sem.at[4]).start()
        return prods + nt(cot[:, at], nn(pick_x, z).astype(BF16))

    prods = lax.fori_loop(0, nb, combine, jnp.zeros((tdev, half), F32))
    total = jnp.sum(jnp.where(here, prods, 0.0), axis=0, keepdims=True)
    top, mid, low = pieces(jnp.where(slot, total, 0.0))
    ggrad[...] = nt(top, spread) + nt(mid, spread) + nt(low, spread)
    for store in stores:
        store.wait()
    pltpu.make_async_copy(mixed, mixed_out, out_sem.at[3]).wait()
    pltpu.make_async_copy(tgrad, tgrad_out, out_sem.at[4]).wait()
    for copy in sends:
        copy.wait_send()
    sent(sbuf, cb_send)


def hand_on(*refs):
    count = (len(refs) - 1) // 2
    copies = [
        pltpu.make_async_copy(refs[i], refs[count + i], refs[-1].at[i]) for i in range(count)
    ]
    for copy in copies:
        copy.start()
    for copy in copies:
        copy.wait()


def body(geo, tokens, cotangent, picks, gates, w_gate, w_up, w_down):
    nx, nzh, nzl, ny, nc = geo
    ne, slots = picks.shape[1], picks.shape[2]
    nb = nx * nzh
    n = nb * ne
    tdev, model = tokens.shape
    wide, ff = w_gate.shape[1], w_gate.shape[2]
    half, hw = ne * 4, 3 * ff // 2
    vm = pl.BlockSpec(memory_space=pltpu.VMEM)
    hbm = pl.BlockSpec(memory_space=pl.ANY)
    far = pl.BlockSpec(memory_space=pltpu.HBM)
    results = (
        jax.ShapeDtypeStruct((tdev, model), BF16),
        jax.ShapeDtypeStruct((tdev, model), BF16),
        jax.ShapeDtypeStruct((slots, ne), F32),
        jax.ShapeDtypeStruct((wide, ff), BF16),
        jax.ShapeDtypeStruct((wide, ff), BF16),
        jax.ShapeDtypeStruct((ff, wide), BF16),
    )
    outs = pl.pallas_call(
        functools.partial(kernel, geo),
        out_shape=results,
        in_specs=[far, far, vm, vm, far, far, far],
        out_specs=(hbm, hbm, vm, hbm, hbm, hbm),
        scratch_shapes=[
            pltpu.VMEM((tdev, model), BF16),
            pltpu.VMEM((tdev, model), BF16),
            pltpu.VMEM((wide, ff), BF16),
            pltpu.VMEM((wide, ff), BF16),
            pltpu.VMEM((ff, wide), BF16),
            pltpu.VMEM((tdev, model), BF16),
            pltpu.VMEM((tdev, model), BF16),
            pltpu.VMEM((wide, ff), BF16),
            pltpu.VMEM((wide, ff), BF16),
            pltpu.VMEM((ff, wide), BF16),
            pltpu.VMEM((n, 8, wide), BF16),
            pltpu.VMEM((n, 8, wide), BF16),
            pltpu.VMEM((nb, half, wide), BF16),
            pltpu.VMEM((nb, half, wide), BF16),
            pltpu.VMEM((nb, 2, half, hw), BF16),
            pltpu.VMEM((2, 2, 2, half, hw), BF16),
            pltpu.VMEM((2, 2, half, hw), BF16),
            pltpu.VMEM((2, 2, half, hw), BF16),
            pltpu.VMEM((2, 2, half, hw), BF16),
            pltpu.VMEM((2, 2, half, hw), BF16),
            pltpu.VMEM((nb, 2, half, hw), BF16),
            pltpu.VMEM((n, 8, wide), BF16),
            pltpu.SemaphoreType.DMA((5,)),
            pltpu.SemaphoreType.DMA((5,)),
            pltpu.SemaphoreType.DMA,
            pltpu.SemaphoreType.DMA((nb,)),
            pltpu.SemaphoreType.DMA((2, 2, 3)),
            pltpu.SemaphoreType.DMA((2, 2, 3)),
            pltpu.SemaphoreType.DMA((2, 2)),
            pltpu.SemaphoreType.DMA((2, 2)),
            pltpu.SemaphoreType.DMA((2, 2, 3)),
            pltpu.SemaphoreType.DMA((2, 2, 3)),
            pltpu.SemaphoreType.DMA,
            pltpu.SemaphoreType.DMA((nb,)),
        ],
        compiler_params=pltpu.CompilerParams(
            collective_id=0, has_side_effects=True, vmem_limit_bytes=46 * 1024 * 1024
        ),
        name="moe",
    )(
        *(
            pltpu.with_memory_space_constraint(v, pltpu.HBM)
            for v in (tokens, cotangent, picks[0].T, gates[0].T, w_gate[0], w_up[0], w_down[0])
        ),
    )
    outs = pl.pallas_call(
        hand_on,
        out_shape=results,
        in_specs=[hbm] * 6,
        out_specs=(hbm,) * 6,
        scratch_shapes=[pltpu.SemaphoreType.DMA((6,))],
        compiler_params=pltpu.CompilerParams(vmem_limit_bytes=12 * 1024 * 1024),
        name="hand_on",
    )(*outs)
    mixed, tgrad, ggrad, gwg, gwu, gwd = outs
    return (mixed, tgrad, ggrad.T[None], gwg[None], gwu[None], gwd[None])


def solution(mesh):
    ne = mesh.shape["expert"]
    geo = (4, 2, 4, 4, 2) if ne == 32 else (4, 2, 1, 1, ne)
    return jax.shard_map(
        functools.partial(body, geo),
        mesh=mesh,
        in_specs=(
            P(("dp", "expert"), None),
            P(("dp", "expert"), None),
            P(("dp", "expert"), None, None),
            P(("dp", "expert"), None, None),
            P("expert", "dp", None),
            P("expert", "dp", None),
            P("expert", None, "dp"),
        ),
        out_specs=(
            P(("dp", "expert"), None),
            P(("dp", "expert"), None),
            P(("dp", "expert"), None, None),
            P("expert", "dp", None),
            P("expert", "dp", None),
            P("expert", None, "dp"),
        ),
        check_vma=False,
    )
```
